32 devices in a mesh: samp: 8 (over y, x, core), cent: 4 (over z).
Axes of the slice: x: 2, y: 2, z: 4, core: 2. Of those that a mesh axis runs over, the one named last changes fastest.
Arguments:
- embeddings: float32 [16384, 1024], P(('samp', 'cent')), may hold values from -40 to 40
- assignment: int32 [16384], P(('samp', 'cent')), may hold values from 0 to 2047, as said below
- owner_map: int32 [2048], replicated, may hold values from 0 to 31, as said below
Outputs:
- centroid: float32 [2048, 1024], P(('samp', 'cent'))
- representative: float32 [2048, 1024], P(('samp', 'cent'))
- keep_weight: float32 [16384], P(('samp', 'cent'))
The draws below stay inside these ranges and needn't reach their ends.
Inputs may be any that keep to these rules, and one draw needn't show every extreme that they name: `owner_map`: every device index, samp-major, owns exactly 64 clusters. `assignment`: of the 512 rows of one device, at most 64 lie in clusters owned by any one device; in every draw some device owns clusters that hold exactly 64 rows of every device.
All inputs are finite; a program needn't handle non-finite values.
Results may differ from the reference program's by a relative error of at most 0.0034.
Values may be sent and summed in bfloat16 or wider, within the bound.
A program may use at most 64 MiB of HBM per device.

```python
import jax
import jax.numpy as jnp
from jax import lax

D = 1024
ROW_DEV = 512
K_DEV = 64
ROWS = 16384
K = 2048
CAP = 64


def shared_layout(key):
    device_count = ROWS // ROW_DEV
    cluster_perm = jax.random.permutation(jax.random.fold_in(key, 11), K)
    owner_values = (cluster_perm // K_DEV).astype(jnp.int32)
    inverse_perm = jnp.argsort(cluster_perm, stable=True).astype(jnp.int32)
    hottest = jax.random.randint(jax.random.fold_in(key, 12), (), 0, device_count)
    block_keys = jax.random.split(jax.random.fold_in(key, 13), device_count)

    def one_block(block_key):
        first_key, second_key, third_key, fourth_key = jax.random.split(block_key, 4)
        other_slots = jax.random.permutation(first_key, (device_count - 1) * CAP)[:ROW_DEV - CAP] // CAP
        other_slots = other_slots + (other_slots >= hottest).astype(jnp.int32)
        targets = jnp.concatenate([jnp.full((CAP,), hottest, jnp.int32), other_slots.astype(jnp.int32)])
        targets = jax.random.permutation(second_key, targets)
        local_rank = jnp.minimum(jax.random.randint(third_key, (ROW_DEV,), 0, K_DEV), jax.random.randint(fourth_key, (ROW_DEV,), 0, K_DEV))
        return inverse_perm[targets * K_DEV + local_rank]
    chosen = jax.vmap(one_block)(block_keys).reshape(ROWS).astype(jnp.int32)
    return (owner_values, chosen)


def draw_owner_map(key, part):
    return shared_layout(key)[0]


def draw_assignment(key, part):
    return shared_layout(key)[1]


def draw_embeddings(key, part):
    chosen = shared_layout(key)[1]
    table = jax.random.normal(jax.random.fold_in(key, 21), (K, D), jnp.float32)
    strength = jax.random.uniform(jax.random.fold_in(key, 22), (ROWS, 1), jnp.float32, 0.3, 3.0)
    noise = jax.random.normal(jax.random.fold_in(key, 23), (ROWS, D), jnp.float32)
    values = strength * table[chosen] + noise
    return jnp.clip(values, -40.0, 40.0)


def setup_inputs(seed: int = 0) -> dict:
    streams_of = jax.random.split(jax.random.key(seed), 4)
    embeddings = draw_embeddings(jax.random.fold_in(streams_of[3], 71), 0)
    assignment = draw_assignment(jax.random.fold_in(streams_of[3], 71), 0)
    owner_map = draw_owner_map(jax.random.fold_in(streams_of[3], 71), 0)
    return {"embeddings": embeddings, "assignment": assignment, "owner_map": owner_map}


EPSILON = 1e-06
SHARPNESS = 8.0

def reference(embeddings, assignment, owner_map):
    unit_rows = (embeddings * lax.rsqrt(lax.optimization_barrier(jnp.sum(embeddings * embeddings, axis=1, keepdims=True)) + EPSILON)).astype(jnp.bfloat16)
    unit_wide = lax.optimization_barrier(unit_rows).astype(jnp.float32)
    cluster_sums = jax.ops.segment_sum(unit_wide, assignment, num_segments=K)
    sum_squares = lax.optimization_barrier(jnp.sum(cluster_sums * cluster_sums, axis=1))
    row_order = jnp.argsort(assignment, stable=True).astype(jnp.int32)
    sorted_units = unit_rows[row_order]
    sorted_ids = assignment[row_order]
    member_counts = jax.ops.segment_sum(jnp.ones((ROWS,), jnp.int32), assignment, num_segments=K).astype(jnp.int32)
    seg_starts = jnp.concatenate([jnp.zeros((1,), jnp.int32), jnp.cumsum(member_counts).astype(jnp.int32)])
    block_size = 128

    def score_block(block_index):
        block_rows = lax.dynamic_slice_in_dim(sorted_units, block_index * block_size, block_size)
        block_ids = lax.dynamic_slice_in_dim(sorted_ids, block_index * block_size, block_size)
        lower_bound = seg_starts[block_ids[0]]
        upper_bound = seg_starts[block_ids[block_size - 1] + 1]
        first_col = (lower_bound // block_size).astype(jnp.int32)
        last_col = ((upper_bound + block_size - 1) // block_size).astype(jnp.int32)

        def column_step(column_index, totals):
            columns = lax.dynamic_slice_in_dim(sorted_units, column_index * block_size, block_size)
            column_ids = lax.dynamic_slice_in_dim(sorted_ids, column_index * block_size, block_size)
            gram = jnp.dot(block_rows, columns.T, preferred_element_type=jnp.float32)
            same_cluster = block_ids[:, None] == column_ids[None, :]
            similar = totals[0] + lax.optimization_barrier(jnp.sum(jnp.where(same_cluster, gram, 0.0), axis=1))
            density = totals[1] + lax.optimization_barrier(jnp.sum(jnp.where(same_cluster, jnp.exp(SHARPNESS * (gram - 1.0)), 0.0), axis=1))
            return (similar, density)
        empty = jnp.zeros((block_size,), jnp.float32)
        return lax.fori_loop(first_col, last_col, column_step, (empty, empty))
    similar, density = lax.map(score_block, jnp.arange(ROWS // block_size, dtype=jnp.int32))
    similar = similar.reshape(ROWS)
    density = density.reshape(ROWS)
    inverse_norm = lax.rsqrt(sum_squares + EPSILON)[sorted_ids]
    spread = 1.0 - similar * inverse_norm
    sorted_weight = jnp.exp(spread) / density
    keep_weight = jnp.zeros((ROWS,), jnp.float32).at[row_order].set(sorted_weight)
    rounded_weight = lax.optimization_barrier(sorted_weight.astype(jnp.bfloat16)).astype(jnp.float32)
    weighted_sums = jax.ops.segment_sum(rounded_weight[:, None] * sorted_units.astype(jnp.float32), sorted_ids, num_segments=K)
    centroid = cluster_sums * lax.rsqrt(sum_squares + EPSILON)[:, None]
    representative = weighted_sums * lax.rsqrt(lax.optimization_barrier(jnp.sum(weighted_sums * weighted_sums, axis=1, keepdims=True)) + EPSILON)
    cluster_order = jnp.argsort(owner_map, stable=True).astype(jnp.int32)
    return (centroid[cluster_order], representative[cluster_order], keep_weight)
```

```python
import functools

import jax
import jax.numpy as jnp
from jax import lax
from jax.experimental import pallas as pl
from jax.experimental.pallas import tpu as pltpu
from jax.sharding import PartitionSpec as P

EPSILON = 1e-06
SHARPNESS = 8.0
LANES = 128
BF = jnp.bfloat16
F32 = jnp.float32
MESH = pl.DeviceIdType.MESH


def iota(shape, axis):
    return lax.broadcasted_iota(jnp.int32, shape, axis)


def row_dot(a, b):
    return lax.dot_general(a, b, (((1,), (1,)), ((), ())), preferred_element_type=F32)


def pack_kernel(devices, near, pool, emb_ref, assign_ref, owner_ref, send_ref, pool_ref, lab_ref, meta_ref):
    rows = emb_ref.shape[0]
    clusters = owner_ref.shape[1]
    upper = (iota((rows, rows), 0) < iota((rows, rows), 1)).astype(BF)
    owner = owner_ref[...]
    owner_hot = (iota((devices, clusters), 0) == owner).astype(F32)
    base = jnp.zeros((devices, 1), F32)
    ranks = []
    for start in range(0, clusters, rows):
        part = owner_hot[:, start:start + rows]
        before = jnp.dot(part.astype(BF), upper, preferred_element_type=F32) + base
        ranks.append(jnp.sum(part * before, axis=0, keepdims=True))
        base = base + jnp.sum(part, axis=1, keepdims=True)
    rank = jnp.concatenate(ranks, axis=1)
    assign = assign_ref[...]
    pick = (iota((clusters, rows), 0) == assign).astype(BF)
    which = iota((8, clusters), 0)
    table = jnp.where(which == 0, owner.astype(F32), jnp.where(which == 1, rank, 0.0)).astype(BF)
    found = jnp.dot(table, pick, preferred_element_type=F32)
    dest = found[0:1, :].astype(jnp.int32)
    label = found[1:2, :] + 1.0
    dest_hot = (iota((devices, rows), 0) == dest).astype(F32)
    before = jnp.dot(dest_hot.astype(BF), upper, preferred_element_type=F32)
    within = jnp.sum(dest_hot * before, axis=0, keepdims=True)
    over = (within >= near).astype(F32)
    over_before = jnp.dot(
        jnp.broadcast_to(over, (8, rows)).astype(BF), upper, preferred_element_type=F32
    )[0:1, :]
    excess = jnp.sum(over, axis=1, keepdims=True) > pool
    within = within.astype(jnp.int32)
    is_over = over > 0.0
    pool_at = over_before.astype(jnp.int32)
    column = jnp.where(is_over, jnp.minimum(near + pool_at, LANES - 2), within)
    col_hot = (iota((LANES, rows), 0) == column).astype(BF)
    labels = row_dot((dest_hot * label).astype(BF), col_hot)
    lane = iota((devices, LANES), 1)
    lab_ref[:, 0, :] = jnp.where(lane == LANES - 1, excess.astype(F32), labels)
    meta_ref[...] = jnp.where(iota((8, rows), 0) == 0, dest, column)
    emb = emb_ref[...]
    unit = (emb * lax.rsqrt(jnp.sum(emb * emb, axis=1, keepdims=True) + EPSILON)).astype(BF)
    slot = jnp.where(is_over, -1, dest * near + within)
    step = devices * near // 4
    for start in range(0, devices * near, step):
        hot = (iota((step, rows), 0) + start == slot).astype(BF)
        out = jnp.dot(hot, unit, preferred_element_type=F32).astype(BF)
        send_ref[start // near:(start + step) // near] = out.reshape(step // near, near, -1)
    pool_hot = (iota((pool, rows), 0) == jnp.where(is_over, pool_at, -1)).astype(BF)
    pool_ref[...] = jnp.dot(pool_hot, unit, preferred_element_type=F32).astype(BF)


def who(n_cent, index):
    return (index // n_cent, index % n_cent)


def enter(n_samp, n_cent, me):
    devices = n_samp * n_cent
    barrier = pltpu.get_barrier_semaphore()

    def greet(k, _):
        pl.semaphore_signal(
            barrier, inc=1, device_id=who(n_cent, (me + k) % devices), device_id_type=MESH
        )
        return 0

    lax.fori_loop(1, devices, greet, 0)
    pl.semaphore_wait(barrier, devices - 1)


def exchange_kernel(
    n_samp, n_cent, send_ref, pool_ref, lab_ref, recv_ref, pools_ref, labs_ref,
    own_sem, row_out, row_in, lab_out, lab_in, near_out, near_in, far_out, far_in,
):
    devices = n_samp * n_cent
    samp = lax.axis_index("samp")
    cent = lax.axis_index("cent")
    me = samp * n_cent + cent
    own = [
        pltpu.make_async_copy(send_ref.at[me], recv_ref.at[me], own_sem.at[0]),
        pltpu.make_async_copy(lab_ref.at[me], labs_ref.at[me], own_sem.at[1]),
        pltpu.make_async_copy(pool_ref, pools_ref.at[samp, cent], own_sem.at[2]),
    ]
    for copy in own:
        copy.start()
    enter(n_samp, n_cent, me)

    def near_copy(k, slot):
        return pltpu.make_async_remote_copy(
            pool_ref, pools_ref.at[samp, slot], near_out.at[k], near_in.at[slot],
            device_id=(samp, (cent + k) % n_cent), device_id_type=MESH,
        )

    def lab_copy(k, slot):
        peer = (me + k) % devices
        return pltpu.make_async_remote_copy(
            lab_ref.at[peer], labs_ref.at[slot], lab_out.at[k], lab_in.at[slot],
            device_id=who(n_cent, peer), device_id_type=MESH,
        )

    def row_copy(k, slot):
        peer = (me + k) % devices
        return pltpu.make_async_remote_copy(
            send_ref.at[peer], recv_ref.at[slot], row_out.at[k], row_in.at[slot],
            device_id=who(n_cent, peer), device_id_type=MESH,
        )

    def far_copy(k, slot):
        return pltpu.make_async_remote_copy(
            pools_ref.at[samp], pools_ref.at[slot], far_out.at[k], far_in.at[slot],
            device_id=((samp + k) % n_samp, cent), device_id_type=MESH,
        )

    def loop(count, body):
        def step(k, _):
            body(k)
            return 0
        lax.fori_loop(1, count, step, 0)

    loop(n_cent, lambda k: near_copy(k, cent).start())
    loop(devices, lambda k: row_copy(k, me).start())
    loop(devices, lambda k: lab_copy(k, me).start())
    own[2].wait()
    loop(n_cent, lambda k: near_copy(k, (cent + k) % n_cent).wait_recv())
    loop(n_samp, lambda k: far_copy(k, samp).start())
    own[0].wait()
    own[1].wait()
    loop(n_cent, lambda k: near_copy(k, cent).wait_send())
    loop(devices, lambda k: row_copy(k, me).wait_send())
    loop(devices, lambda k: lab_copy(k, me).wait_send())
    loop(n_samp, lambda k: far_copy(k, samp).wait_send())
    loop(devices, lambda k: lab_copy(k, (me + k) % devices).wait_recv())
    loop(devices, lambda k: row_copy(k, (me + k) % devices).wait_recv())
    loop(n_samp, lambda k: far_copy(k, (samp + k) % n_samp).wait_recv())


def return_kernel(n_samp, n_cent, out_ref, back_ref, own_sem, out_sem, in_sem):
    devices = n_samp * n_cent
    me = lax.axis_index("samp") * n_cent + lax.axis_index("cent")
    own = pltpu.make_async_copy(out_ref.at[me], back_ref.at[me], own_sem)
    own.start()
    enter(n_samp, n_cent, me)

    def copy(k, slot):
        peer = (me + k) % devices
        return pltpu.make_async_remote_copy(
            out_ref.at[peer], back_ref.at[slot], out_sem.at[k], in_sem.at[slot],
            device_id=who(n_cent, peer), device_id_type=MESH,
        )

    def loop(body):
        def step(k, _):
            body(k)
            return 0
        lax.fori_loop(1, devices, step, 0)

    loop(lambda k: copy(k, me).start())
    own.wait()
    loop(lambda k: copy(k, me).wait_send())
    loop(lambda k: copy(k, (me + k) % devices).wait_recv())


def score_kernel(per_owner, near_ref, far_ref, tags_ref, cent_ref, rep_ref, weight_ref, x_ref, col_ref, dens_ref):
    half = near_ref.shape[0]
    slots = half + far_ref.shape[0]
    x_ref[0:half, :] = near_ref[...]
    x_ref[half:, :] = far_ref[...]
    tags = tags_ref[...]
    for start in range(0, slots, LANES):
        chunk = jnp.broadcast_to(tags[:, start:start + LANES], (LANES, LANES))
        col_ref[start:start + LANES, :] = jnp.transpose(chunk)
    member = tags == (iota((per_owner, slots), 0) + 1).astype(F32)
    member_bf = member.astype(BF)
    sums = jnp.dot(member_bf, x_ref[...], preferred_element_type=F32)
    scale = lax.rsqrt(jnp.sum(sums * sums, axis=1, keepdims=True) + EPSILON)
    centroid = sums * scale
    cent_ref[...] = centroid
    high = centroid.astype(BF)
    low = (centroid - high.astype(F32)).astype(BF)
    block = 256
    chunk = 512

    def column(j, _):
        at = pl.multiple_of(j * block, block)
        right = x_ref[pl.ds(at, block), :]
        tag = tags_ref[:, pl.ds(at, block)]

        def inner(i, total):
            top = pl.multiple_of(i * chunk, chunk)
            gram = row_dot(x_ref[pl.ds(top, chunk), :], right)
            left = col_ref[pl.ds(top, chunk), :]
            same = jnp.concatenate([left] * (block // LANES), axis=1) == tag
            part = jnp.where(same, jnp.exp(SHARPNESS * (gram - 1.0)), 0.0)
            return total + jnp.sum(part, axis=0, keepdims=True)

        dens_ref[:, pl.ds(at, block)] = lax.fori_loop(
            0, slots // chunk, inner, jnp.zeros((1, block), F32)
        )
        return 0

    lax.fori_loop(0, slots // block, column, 0)
    towards = row_dot(high, x_ref[...]) + row_dot(low, x_ref[...])
    similar = jnp.sum(jnp.where(member, towards, 0.0), axis=0, keepdims=True)
    valid = tags > 0.0
    density = jnp.where(valid, dens_ref[...], 1.0)
    weight = jnp.where(valid, jnp.exp(1.0 - similar) / density, 0.0)
    weight_ref[...] = weight
    mixed = jnp.dot(
        jnp.where(member, weight, 0.0).astype(BF), x_ref[...], preferred_element_type=F32
    )
    rep_ref[...] = mixed * lax.rsqrt(jnp.sum(mixed * mixed, axis=1, keepdims=True) + EPSILON)


def pick_kernel(back_ref, meta_ref, keep_ref):
    devices = back_ref.shape[0]
    rows = meta_ref.shape[1]
    meta = meta_ref[...]
    dest_hot = (iota((devices, rows), 0) == meta[0:1, :]).astype(F32)
    spread = lax.dot_general(
        back_ref[:, 0, :], dest_hot, (((0,), (0,)), ((), ())),
        preferred_element_type=F32, precision=lax.Precision.HIGHEST,
    )
    hit = iota((LANES, rows), 0) == meta[1:2, :]
    keep_ref[...] = jnp.sum(jnp.where(hit, spread, 0.0), axis=0, keepdims=True)


def all_pairs(arrived, arrived_tags, validity, block_size):
    slot_count, feature_width = arrived.shape
    block_count = slot_count // block_size

    def score_block(pieces):
        block_rows, block_tags = pieces
        gram = jnp.einsum("rd,qd->rq", block_rows, arrived, preferred_element_type=jnp.float32)
        same_cluster = (block_tags[:, None] == arrived_tags[None, :]) & validity[None, :]
        similar = jnp.sum(jnp.where(same_cluster, gram, 0.0), axis=1)
        density = jnp.sum(jnp.where(same_cluster, jnp.exp(SHARPNESS * (gram - 1.0)), 0.0), axis=1)
        return (similar, density)

    similar, density = lax.map(
        score_block,
        (
            arrived.reshape(block_count, block_size, feature_width),
            arrived_tags.reshape(block_count, block_size),
        ),
    )
    return (similar.reshape(slot_count), density.reshape(slot_count))


def full_capacity(embeddings, assignment, owner_map):
    row_count, feature_width = embeddings.shape
    devices = lax.axis_size("samp") * lax.axis_size("cent")
    clusters = owner_map.shape[0]
    per_owner = clusters // devices
    capacity = 4 * row_count // devices
    slot_count = devices * capacity
    unit_rows = (
        embeddings * lax.rsqrt(jnp.sum(embeddings * embeddings, axis=1, keepdims=True) + EPSILON)
    ).astype(jnp.bfloat16)
    destination = owner_map[assignment]
    cluster_order = jnp.argsort(owner_map, stable=True)
    position = (
        jnp.zeros((clusters,), jnp.int32)
        .at[cluster_order]
        .set(jnp.arange(clusters, dtype=jnp.int32))
    )
    local_rank = position[assignment] - destination * per_owner
    dest_onehot = (destination[:, None] == jnp.arange(devices, dtype=jnp.int32)[None, :]).astype(
        jnp.int32
    )
    within_rank = jnp.sum(jnp.cumsum(dest_onehot, axis=0) * dest_onehot, axis=1) - 1
    slot_index = destination * capacity + within_rank
    outgoing = jnp.zeros((slot_count, feature_width), jnp.bfloat16).at[slot_index].set(unit_rows)
    labels = (
        jnp.zeros((slot_count,), jnp.bfloat16)
        .at[slot_index]
        .set((local_rank + 1).astype(jnp.bfloat16))
    )
    arrived, arrived_labels = (
        lax.all_to_all(outgoing, ("samp", "cent"), split_axis=0, concat_axis=0, tiled=True),
        lax.all_to_all(labels, ("samp", "cent"), split_axis=0, concat_axis=0, tiled=True),
    )
    arrived_tags = arrived_labels.astype(jnp.int32) - 1
    validity = arrived_tags >= 0
    block_size = min(512, slot_count)
    similar, density = all_pairs(arrived, arrived_tags, validity, block_size)
    member = arrived_tags[None, :] == jnp.arange(per_owner, dtype=jnp.int32)[:, None]
    member_bf = member.astype(jnp.bfloat16)
    cluster_sums = jnp.dot(member_bf, arrived, preferred_element_type=jnp.float32)
    inverse_norm = lax.rsqrt(jnp.sum(cluster_sums * cluster_sums, axis=1) + EPSILON)
    row_scale = jnp.sum(member.astype(jnp.float32) * inverse_norm[:, None], axis=0)
    spread = 1.0 - similar * row_scale
    weight = jnp.where(validity, jnp.exp(spread) / jnp.where(validity, density, 1.0), 0.0)
    weighted = jnp.dot(
        member_bf * weight.astype(jnp.bfloat16)[None, :],
        arrived,
        preferred_element_type=jnp.float32,
    )
    centroid = cluster_sums * inverse_norm[:, None]
    representative = weighted * lax.rsqrt(
        jnp.sum(weighted * weighted, axis=1, keepdims=True) + EPSILON
    )
    returned = lax.all_to_all(weight, ("samp", "cent"), split_axis=0, concat_axis=0, tiled=True)
    keep_weight = returned[slot_index]
    return (centroid, representative, keep_weight)


def on_device(embeddings, assignment, owner_map):
    rows, width = embeddings.shape
    n_samp = lax.axis_size("samp")
    n_cent = lax.axis_size("cent")
    devices = n_samp * n_cent
    clusters = owner_map.shape[0]
    per_owner = clusters // devices
    capacity = 4 * rows // devices
    near = capacity // 2
    pool = capacity - near
    vmem = pl.BlockSpec(memory_space=pltpu.VMEM)
    anywhere = pl.BlockSpec(memory_space=pl.ANY)
    shape = jax.ShapeDtypeStruct
    dma = pltpu.SemaphoreType.DMA
    send, pooled, labels, meta = pl.pallas_call(
        functools.partial(pack_kernel, devices, near, pool),
        out_shape=(
            shape((devices, near, width), BF),
            shape((pool, width), BF),
            shape((devices, 1, LANES), F32),
            shape((8, rows), jnp.int32),
        ),
        in_specs=[vmem] * 3,
        out_specs=(vmem,) * 4,
        name="pack",
    )(embeddings, assignment.reshape(1, rows), owner_map.reshape(1, clusters))
    arrived, pools, tags = pl.pallas_call(
        functools.partial(exchange_kernel, n_samp, n_cent),
        out_shape=(
            shape((devices, near, width), BF),
            shape((n_samp, n_cent, pool, width), BF),
            shape((devices, 1, LANES), F32),
        ),
        in_specs=[anywhere] * 3,
        out_specs=(anywhere,) * 3,
        scratch_shapes=[
            dma((3,)), dma((devices,)), dma((devices,)), dma((devices,)), dma((devices,)),
            dma((n_cent,)), dma((n_cent,)), dma((n_samp,)), dma((n_samp,)),
        ],
        compiler_params=pltpu.CompilerParams(collective_id=0, has_side_effects=True),
        name="exchange",
    )(send, pooled, labels)
    tags = tags[:, 0, :]

    def fast(embeddings, assignment, owner_map, arrived, pools, tags, meta):
        half = devices * near
        slots = half + devices * pool
        tag_row = jnp.concatenate(
            [tags[:, :near].reshape(1, half), tags[:, near:capacity].reshape(1, slots - half)], axis=1
        )
        centroid, representative, weight = pl.pallas_call(
            functools.partial(score_kernel, per_owner),
            out_shape=(
                shape((per_owner, width), F32),
                shape((per_owner, width), F32),
                shape((1, slots), F32),
            ),
            in_specs=[vmem] * 3,
            out_specs=(vmem,) * 3,
            scratch_shapes=[
                pltpu.VMEM((slots, width), BF),
                pltpu.VMEM((slots, LANES), F32),
                pltpu.VMEM((1, slots), F32),
            ],
            name="score",
        )(arrived.reshape(half, width), pools.reshape(slots - half, width), tag_row)
        out = jnp.concatenate(
            [
                weight[:, :half].reshape(devices, near),
                weight[:, half:].reshape(devices, pool),
                jnp.zeros((devices, LANES - capacity), F32),
            ],
            axis=1,
        )
        back = pl.pallas_call(
            functools.partial(return_kernel, n_samp, n_cent),
            out_shape=shape((devices, 1, LANES), F32),
            in_specs=[vmem],
            out_specs=vmem,
            scratch_shapes=[dma, dma((devices,)), dma((devices,))],
            compiler_params=pltpu.CompilerParams(collective_id=1, has_side_effects=True),
            name="give_back",
        )(out.reshape(devices, 1, LANES))
        keep = pl.pallas_call(
            pick_kernel,
            out_shape=shape((1, rows), F32),
            in_specs=[vmem] * 2,
            out_specs=vmem,
            name="pick",
        )(back, meta)
        return centroid, representative, keep.reshape(rows)

    def slow(embeddings, assignment, owner_map, arrived, pools, tags, meta):
        return full_capacity(embeddings, assignment, owner_map)

    spilled = jnp.max(tags[:, LANES - 1]) > 0.0
    return lax.cond(
        spilled, slow, fast, embeddings, assignment, owner_map, arrived, pools, tags, meta
    )


def solution(mesh):
    in_specs = (P(("samp", "cent"), None), P(("samp", "cent")), P())
    out_specs = (P(("samp", "cent"), None), P(("samp", "cent"), None), P(("samp", "cent")))
    return jax.shard_map(
        on_device, mesh=mesh, in_specs=in_specs, out_specs=out_specs, check_vma=False
    )
```

```python
import functools

import jax
import jax.numpy as jnp
from jax import lax
from jax.experimental import pallas as pl
from jax.experimental.pallas import tpu as pltpu
from jax.sharding import PartitionSpec as P

EPSILON = 1e-06
SHARPNESS = 8.0
LANES = 128
SPILL = 65536.0
BF = jnp.bfloat16
F32 = jnp.float32
MESH = pl.DeviceIdType.MESH


def iota(shape, axis):
    return lax.broadcasted_iota(jnp.int32, shape, axis)


def row_dot(a, b):
    return lax.dot_general(a, b, (((1,), (1,)), ((), ())), preferred_element_type=F32)


def pack_kernel(devices, n_cent, near, pool, emb_ref, assign_ref, owner_ref, send_ref, pool_ref, lab_ref, meta_ref):
    rows = emb_ref.shape[0]
    clusters = owner_ref.shape[1]
    upper = (iota((rows, rows), 0) < iota((rows, rows), 1)).astype(BF)
    owner = owner_ref[...]
    owner_hot = (iota((devices, clusters), 0) == owner).astype(F32)
    base = jnp.zeros((devices, 1), F32)
    ranks = []
    for start in range(0, clusters, rows):
        part = owner_hot[:, start:start + rows]
        before = jnp.dot(part.astype(BF), upper, preferred_element_type=F32) + base
        ranks.append(jnp.sum(part * before, axis=0, keepdims=True))
        base = base + jnp.sum(part, axis=1, keepdims=True)
    rank = jnp.concatenate(ranks, axis=1)
    assign = assign_ref[...]
    pick = (iota((clusters, rows), 0) == assign).astype(BF)
    which = iota((8, clusters), 0)
    table = jnp.where(which == 0, owner.astype(F32), jnp.where(which == 1, rank, 0.0)).astype(BF)
    found = jnp.dot(table, pick, preferred_element_type=F32)
    dest = found[0:1, :].astype(jnp.int32)
    label = found[1:2, :] + 1.0
    dest_hot = (iota((devices, rows), 0) == dest).astype(F32)
    before = jnp.dot(dest_hot.astype(BF), upper, preferred_element_type=F32)
    within = jnp.sum(dest_hot * before, axis=0, keepdims=True)
    over = (within >= near).astype(F32)
    over_before = jnp.dot(
        jnp.broadcast_to(over, (8, rows)).astype(BF), upper, preferred_element_type=F32
    )[0:1, :]
    excess = jnp.sum(over, axis=1, keepdims=True) > pool
    within = within.astype(jnp.int32)
    is_over = over > 0.0
    pool_at = over_before.astype(jnp.int32)
    cent = lax.axis_index("cent")
    lanes = lab_ref.shape[2]
    column = jnp.where(
        is_over, n_cent * near + cent * pool + jnp.minimum(pool_at, pool - 1), cent * near + within
    )
    col_hot = (iota((lanes, rows), 0) == column).astype(BF)
    labels = row_dot((dest_hot * label).astype(BF), col_hot)
    lab_ref[:, 0, :] = labels + jnp.where(excess, SPILL, 0.0)
    meta_ref[...] = jnp.where(iota((8, rows), 0) == 0, dest, column)
    emb = emb_ref[...]
    unit = (emb * lax.rsqrt(jnp.sum(emb * emb, axis=1, keepdims=True) + EPSILON)).astype(BF)
    slot = jnp.where(is_over, -1, dest * near + within)
    step = devices * near // 4
    for start in range(0, devices * near, step):
        hot = (iota((step, rows), 0) + start == slot).astype(BF)
        out = jnp.dot(hot, unit, preferred_element_type=F32).astype(BF)
        send_ref[start // near:(start + step) // near] = out.reshape(step // near, near, -1)
    pool_hot = (iota((pool, rows), 0) == jnp.where(is_over, pool_at, -1)).astype(BF)
    pool_ref[...] = jnp.dot(pool_hot, unit, preferred_element_type=F32).astype(BF)


def who(n_cent, index):
    return (index // n_cent, index % n_cent)


def enter(n_samp, n_cent, me):
    devices = n_samp * n_cent
    barrier = pltpu.get_barrier_semaphore()

    def greet(k, _):
        pl.semaphore_signal(
            barrier, inc=1, device_id=who(n_cent, (me + k) % devices), device_id_type=MESH
        )
        return 0

    lax.fori_loop(1, devices, greet, 0)
    pl.semaphore_wait(barrier, devices - 1)


def dedup_kernel(
    n_samp, n_cent, send_ref, pool_ref, lab_ref, cent_ref, rep_ref, back_ref, tags_ref,
    near_ref, pools_ref, labs_ref, x_ref, col_ref, turn_ref, dens_ref, sums_ref, out_ref,
    own_sem, row_out, row_in, lab_out, lab_in, near_out, near_in, far_out, far_in, back_out, back_in,
):
    samp = lax.axis_index("samp")
    cent = lax.axis_index("cent")
    me = samp * n_cent + cent
    per_owner = cent_ref.shape[0]
    near = near_ref.shape[2]
    pool = pools_ref.shape[2]
    width = x_ref.shape[1]
    split = n_cent * near
    block = n_cent * (near + pool)
    slots = n_samp * block

    def loop(low, high, body):
        def step(k, _):
            body(k)
            return 0
        lax.fori_loop(low, high, step, 0)

    def target(shift, c):
        return ((samp + shift) % n_samp, c)

    def near_copy(c, slot):
        return pltpu.make_async_remote_copy(
            pool_ref, pools_ref.at[0, slot], near_out.at[c], near_in.at[slot],
            device_id=(samp, c), device_id_type=MESH,
        )

    def row_copy(k, c, slot):
        s, t = target(k, c)
        return pltpu.make_async_remote_copy(
            send_ref.at[s * n_cent + t], near_ref.at[k, slot], row_out.at[k, c], row_in.at[k, slot],
            device_id=(s, t), device_id_type=MESH,
        )

    def lab_copy(k, c, slot):
        s, t = target(k, c)
        return pltpu.make_async_remote_copy(
            lab_ref.at[s * n_cent + t], labs_ref.at[k, slot], lab_out.at[k, c], lab_in.at[k, slot],
            device_id=(s, t), device_id_type=MESH,
        )

    def far_copy(k):
        return pltpu.make_async_remote_copy(
            pools_ref.at[0], pools_ref.at[k], far_out.at[k], far_in.at[k],
            device_id=target(k, cent), device_id_type=MESH,
        )

    def back_copy(k, c, slot, at_c):
        s = (samp + n_samp - k) % n_samp
        return pltpu.make_async_remote_copy(
            out_ref.at[k], back_ref.at[slot], back_out.at[k, c], back_in.at[k, at_c],
            device_id=(s, c), device_id_type=MESH,
        )

    def others(k, body):
        if k == 0:
            loop(1, n_cent, lambda c: body((cent + c) % n_cent))
        else:
            loop(0, n_cent, lambda c: body((cent + c) % n_cent))

    own = [
        pltpu.make_async_copy(send_ref.at[me], near_ref.at[0, cent], own_sem.at[0]),
        pltpu.make_async_copy(lab_ref.at[me], labs_ref.at[0, cent], own_sem.at[1]),
        pltpu.make_async_copy(pool_ref, pools_ref.at[0, cent], own_sem.at[2]),
    ]
    for copy in own:
        copy.start()
    enter(n_samp, n_cent, me)

    def rows_start(k):
        others(k, lambda c: lab_copy(k, c, cent).start())
        others(k, lambda c: row_copy(k, c, cent).start())

    others(0, lambda c: near_copy(c, cent).start())
    rows_start(0)
    rows_start(1)
    turn_ref[...] = jnp.zeros_like(turn_ref)
    own[2].wait()
    others(0, lambda c: near_copy(c, c).wait_recv())
    far_copy(1).start()
    for k in range(2, n_samp):
        rows_start(k)
        far_copy(k).start()
    own[0].wait()
    own[1].wait()
    sums_ref[...] = jnp.zeros_like(sums_ref)
    for k in range(n_samp):
        at = k * block
        others(k, lambda c: lab_copy(k, c, c).wait_recv())
        others(k, lambda c: row_copy(k, c, c).wait_recv())
        if k > 0:
            far_copy(k).wait_recv()
        x_ref[at:at + split, :] = near_ref[k].reshape(split, width)
        x_ref[at + split:at + block, :] = pools_ref[k].reshape(block - split, width)
        tag = jnp.sum(labs_ref[k], axis=0)
        tags_ref[k] = tag
        for start in range(0, block, LANES):
            chunk = jnp.broadcast_to(tag[:, start:start + LANES], (LANES, LANES))
            col_ref[at + start:at + start + LANES, :] = jnp.transpose(chunk)
        fresh = x_ref[at:at + block, :]
        member = (tag == (iota((per_owner, block), 0) + 1).astype(F32)).astype(BF)
        sums_ref[...] += jnp.dot(member, fresh, preferred_element_type=F32)

        def piece(top, height):
            gram = row_dot(x_ref[pl.ds(top, height), :], fresh)
            left = col_ref[pl.ds(top, height), :]
            same = jnp.concatenate([left] * (block // LANES), axis=1) == tag
            return jnp.where(same, jnp.exp(SHARPNESS * (gram - 1.0)), 0.0)

        def both(top, height):
            part = piece(top, height)
            folded = part[:, 0:LANES]
            for start in range(LANES, block, LANES):
                folded = folded + part[:, start:start + LANES]
            turn_ref[pl.ds(top, height), :] += folded
            return jnp.sum(part, axis=0, keepdims=True)

        total = jnp.sum(piece(at, block), axis=0, keepdims=True)
        if k >= 2:
            total = lax.fori_loop(
                0, k // 2,
                lambda j, t: t + both(pl.multiple_of(j * 2 * block, 2 * block), 2 * block),
                total,
            )
        if k % 2:
            total = total + both((k - 1) * block, block)
        dens_ref[k] = total
    sums = sums_ref[...]
    scale = lax.rsqrt(jnp.sum(sums * sums, axis=1, keepdims=True) + EPSILON)
    centroid = sums * scale
    cent_ref[...] = centroid
    high = centroid.astype(BF)
    low = (centroid - high.astype(F32)).astype(BF)
    pair = jnp.concatenate([high, low], axis=0)
    for k in range(n_samp):
        at = k * block
        tag = tags_ref[k]
        valid = tag > 0.0
        member = tag == (iota((per_owner, block), 0) + 1).astype(F32)
        towards = row_dot(pair, x_ref[at:at + block, :])
        towards = towards[0:per_owner, :] + towards[per_owner:, :]
        similar = jnp.sum(jnp.where(member, towards, 0.0), axis=0, keepdims=True)
        flipped = []
        for start in range(at, at + block, LANES):
            flipped.append(
                jnp.sum(jnp.transpose(turn_ref[start:start + LANES, :]), axis=0, keepdims=True)
            )
        density = jnp.where(valid, dens_ref[k] + jnp.concatenate(flipped, axis=1), 1.0)
        out_ref[k] = jnp.where(valid, jnp.exp(1.0 - similar) / density, 0.0)
    mine = pltpu.make_async_copy(out_ref.at[0], back_ref.at[me], own_sem.at[3])
    mine.start()
    mine.wait()
    for k in range(n_samp):
        others(k, lambda c: back_copy(k, c, me, cent).start())
    mixed = jnp.zeros(sums_ref.shape, F32)
    for k in range(n_samp):
        member = tags_ref[k] == (iota((per_owner, block), 0) + 1).astype(F32)
        mixed = mixed + jnp.dot(
            jnp.where(member, out_ref[k], 0.0).astype(BF), x_ref[k * block:(k + 1) * block, :],
            preferred_element_type=F32,
        )
    rep_ref[...] = mixed * lax.rsqrt(jnp.sum(mixed * mixed, axis=1, keepdims=True) + EPSILON)
    others(0, lambda c: near_copy(c, cent).wait_send())
    for k in range(n_samp):
        others(k, lambda c: lab_copy(k, c, cent).wait_send())
        others(k, lambda c: row_copy(k, c, cent).wait_send())
        if k > 0:
            far_copy(k).wait_send()
        others(k, lambda c: back_copy(k, c, me, cent).wait_send())
    for k in range(n_samp):
        others(k, lambda c: back_copy(k, c, ((samp + k) % n_samp) * n_cent + c, c).wait_recv())


def pick_kernel(back_ref, meta_ref, keep_ref):
    devices = back_ref.shape[0]
    rows = meta_ref.shape[1]
    meta = meta_ref[...]
    dest_hot = (iota((devices, rows), 0) == meta[0:1, :]).astype(F32)
    spread = lax.dot_general(
        back_ref[:, 0, :], dest_hot, (((0,), (0,)), ((), ())),
        preferred_element_type=F32, precision=lax.Precision.HIGHEST,
    )
    hit = iota((back_ref.shape[2], rows), 0) == meta[1:2, :]
    keep_ref[...] = jnp.sum(jnp.where(hit, spread, 0.0), axis=0, keepdims=True)


def all_pairs(arrived, arrived_tags, validity, block_size):
    slot_count, feature_width = arrived.shape
    block_count = slot_count // block_size

    def score_block(pieces):
        block_rows, block_tags = pieces
        gram = jnp.einsum("rd,qd->rq", block_rows, arrived, preferred_element_type=jnp.float32)
        same_cluster = (block_tags[:, None] == arrived_tags[None, :]) & validity[None, :]
        similar = jnp.sum(jnp.where(same_cluster, gram, 0.0), axis=1)
        density = jnp.sum(jnp.where(same_cluster, jnp.exp(SHARPNESS * (gram - 1.0)), 0.0), axis=1)
        return (similar, density)

    similar, density = lax.map(
        score_block,
        (
            arrived.reshape(block_count, block_size, feature_width),
            arrived_tags.reshape(block_count, block_size),
        ),
    )
    return (similar.reshape(slot_count), density.reshape(slot_count))


def full_capacity(embeddings, assignment, owner_map):
    row_count, feature_width = embeddings.shape
    devices = lax.axis_size("samp") * lax.axis_size("cent")
    clusters = owner_map.shape[0]
    per_owner = clusters // devices
    capacity = 4 * row_count // devices
    slot_count = devices * capacity
    unit_rows = (
        embeddings * lax.rsqrt(jnp.sum(embeddings * embeddings, axis=1, keepdims=True) + EPSILON)
    ).astype(jnp.bfloat16)
    destination = owner_map[assignment]
    cluster_order = jnp.argsort(owner_map, stable=True)
    position = (
        jnp.zeros((clusters,), jnp.int32)
        .at[cluster_order]
        .set(jnp.arange(clusters, dtype=jnp.int32))
    )
    local_rank = position[assignment] - destination * per_owner
    dest_onehot = (destination[:, None] == jnp.arange(devices, dtype=jnp.int32)[None, :]).astype(
        jnp.int32
    )
    within_rank = jnp.sum(jnp.cumsum(dest_onehot, axis=0) * dest_onehot, axis=1) - 1
    slot_index = destination * capacity + within_rank
    outgoing = jnp.zeros((slot_count, feature_width), jnp.bfloat16).at[slot_index].set(unit_rows)
    labels = (
        jnp.zeros((slot_count,), jnp.bfloat16)
        .at[slot_index]
        .set((local_rank + 1).astype(jnp.bfloat16))
    )
    arrived, arrived_labels = (
        lax.all_to_all(outgoing, ("samp", "cent"), split_axis=0, concat_axis=0, tiled=True),
        lax.all_to_all(labels, ("samp", "cent"), split_axis=0, concat_axis=0, tiled=True),
    )
    arrived_tags = arrived_labels.astype(jnp.int32) - 1
    validity = arrived_tags >= 0
    block_size = min(512, slot_count)
    similar, density = all_pairs(arrived, arrived_tags, validity, block_size)
    member = arrived_tags[None, :] == jnp.arange(per_owner, dtype=jnp.int32)[:, None]
    member_bf = member.astype(jnp.bfloat16)
    cluster_sums = jnp.dot(member_bf, arrived, preferred_element_type=jnp.float32)
    inverse_norm = lax.rsqrt(jnp.sum(cluster_sums * cluster_sums, axis=1) + EPSILON)
    row_scale = jnp.sum(member.astype(jnp.float32) * inverse_norm[:, None], axis=0)
    spread = 1.0 - similar * row_scale
    weight = jnp.where(validity, jnp.exp(spread) / jnp.where(validity, density, 1.0), 0.0)
    weighted = jnp.dot(
        member_bf * weight.astype(jnp.bfloat16)[None, :],
        arrived,
        preferred_element_type=jnp.float32,
    )
    centroid = cluster_sums * inverse_norm[:, None]
    representative = weighted * lax.rsqrt(
        jnp.sum(weighted * weighted, axis=1, keepdims=True) + EPSILON
    )
    returned = lax.all_to_all(weight, ("samp", "cent"), split_axis=0, concat_axis=0, tiled=True)
    keep_weight = returned[slot_index]
    return (centroid, representative, keep_weight)


def on_device(embeddings, assignment, owner_map):
    rows, width = embeddings.shape
    n_samp = lax.axis_size("samp")
    n_cent = lax.axis_size("cent")
    devices = n_samp * n_cent
    clusters = owner_map.shape[0]
    per_owner = clusters // devices
    capacity = 4 * rows // devices
    near = capacity // 2
    pool = capacity - near
    vmem = pl.BlockSpec(memory_space=pltpu.VMEM)
    anywhere = pl.BlockSpec(memory_space=pl.ANY)
    shape = jax.ShapeDtypeStruct
    dma = pltpu.SemaphoreType.DMA
    block = n_cent * capacity
    slots = n_samp * block
    send, pooled, labels, meta = pl.pallas_call(
        functools.partial(pack_kernel, devices, n_cent, near, pool),
        out_shape=(
            shape((devices, near, width), BF),
            shape((pool, width), BF),
            shape((devices, 1, block), F32),
            shape((8, rows), jnp.int32),
        ),
        in_specs=[vmem] * 3,
        out_specs=(vmem,) * 4,
        name="pack",
    )(embeddings, assignment.reshape(1, rows), owner_map.reshape(1, clusters))
    centroid, representative, back, tags = pl.pallas_call(
        functools.partial(dedup_kernel, n_samp, n_cent),
        out_shape=(
            shape((per_owner, width), F32),
            shape((per_owner, width), F32),
            shape((devices, 1, block), F32),
            shape((n_samp, 1, block), F32),
        ),
        in_specs=[anywhere] * 3,
        out_specs=(vmem,) * 4,
        scratch_shapes=[
            pltpu.VMEM((n_samp, n_cent, near, width), BF),
            pltpu.VMEM((n_samp, n_cent, pool, width), BF),
            pltpu.VMEM((n_samp, n_cent, 1, block), F32),
            pltpu.VMEM((slots, width), BF),
            pltpu.VMEM((slots, LANES), F32),
            pltpu.VMEM((slots, LANES), F32),
            pltpu.VMEM((n_samp, 1, block), F32),
            pltpu.VMEM((per_owner, width), F32),
            pltpu.VMEM((n_samp, 1, block), F32),
            dma((4,)),
            dma((n_samp, n_cent)), dma((n_samp, n_cent)), dma((n_samp, n_cent)), dma((n_samp, n_cent)),
            dma((n_cent,)), dma((n_cent,)), dma((n_samp,)), dma((n_samp,)),
            dma((n_samp, n_cent)), dma((n_samp, n_cent)),
        ],
        compiler_params=pltpu.CompilerParams(collective_id=0, has_side_effects=True),
        name="dedup",
    )(send, pooled, labels)
    keep = pl.pallas_call(
        pick_kernel,
        out_shape=shape((1, rows), F32),
        in_specs=[vmem] * 2,
        out_specs=vmem,
        name="pick",
    )(back, meta).reshape(rows)

    def fast(embeddings, assignment, owner_map, centroid, representative, keep):
        return centroid, representative, keep

    def slow(embeddings, assignment, owner_map, centroid, representative, keep):
        return full_capacity(embeddings, assignment, owner_map)

    spilled = jnp.max(tags) >= SPILL
    return lax.cond(
        spilled, slow, fast, embeddings, assignment, owner_map, centroid, representative, keep
    )


def solution(mesh):
    in_specs = (P(("samp", "cent"), None), P(("samp", "cent")), P())
    out_specs = (P(("samp", "cent"), None), P(("samp", "cent"), None), P(("samp", "cent")))
    return jax.shard_map(
        on_device, mesh=mesh, in_specs=in_specs, out_specs=out_specs, check_vma=False
    )
```

```python
import functools

import jax
import jax.numpy as jnp
from jax import lax
from jax.experimental import pallas as pl
from jax.experimental.pallas import tpu as pltpu
from jax.sharding import PartitionSpec as P

EPSILON = 1e-06
SHARPNESS = 8.0
LANES = 128
SPILL = 65536.0
BF = jnp.bfloat16
F32 = jnp.float32
MESH = pl.DeviceIdType.MESH


def iota(shape, axis):
    return lax.broadcasted_iota(jnp.int32, shape, axis)


def row_dot(a, b):
    return lax.dot_general(a, b, (((1,), (1,)), ((), ())), preferred_element_type=F32)


def samp_half(shift):
    return (shift // 2) % 2


def pack_kernel(devices, n_cent, near, pool, emb_ref, assign_ref, owner_ref, send_ref, pool_ref, index_ref, lab_ref, meta_ref):
    rows = emb_ref.shape[0]
    clusters = owner_ref.shape[1]
    upper = (iota((rows, rows), 0) < iota((rows, rows), 1)).astype(BF)
    owner = owner_ref[...]
    owner_hot = (iota((devices, clusters), 0) == owner).astype(F32)
    base = jnp.zeros((devices, 1), F32)
    ranks = []
    for start in range(0, clusters, rows):
        part = owner_hot[:, start:start + rows]
        before = jnp.dot(part.astype(BF), upper, preferred_element_type=F32) + base
        ranks.append(jnp.sum(part * before, axis=0, keepdims=True))
        base = base + jnp.sum(part, axis=1, keepdims=True)
    rank = jnp.concatenate(ranks, axis=1)
    assign = assign_ref[...]
    pick = (iota((clusters, rows), 0) == assign).astype(BF)
    which = iota((8, clusters), 0)
    table = jnp.where(which == 0, owner.astype(F32), jnp.where(which == 1, rank, 0.0)).astype(BF)
    found = jnp.dot(table, pick, preferred_element_type=F32)
    dest = found[0:1, :].astype(jnp.int32)
    label = found[1:2, :] + 1.0
    dest_hot = (iota((devices, rows), 0) == dest).astype(F32)
    before = jnp.dot(dest_hot.astype(BF), upper, preferred_element_type=F32)
    within = jnp.sum(dest_hot * before, axis=0, keepdims=True)
    over = (within >= near).astype(F32)
    over_before = jnp.dot(
        jnp.broadcast_to(over, (8, rows)).astype(BF), upper, preferred_element_type=F32
    )[0:1, :]
    excess = jnp.sum(over, axis=1, keepdims=True) > pool
    within = within.astype(jnp.int32)
    is_over = over > 0.0
    pool_at = over_before.astype(jnp.int32)
    samp = lax.axis_index("samp")
    cent = lax.axis_index("cent")
    n_samp = devices // n_cent
    span = n_samp * near
    shift = (dest // n_cent + n_samp - samp) % n_samp
    toward = dest % n_cent
    near_lane = shift * near + within
    pair_lane = (samp_half(shift) * n_cent + cent) * pool + jnp.minimum(pool_at, pool - 1)
    column = jnp.where(is_over, span + pair_lane, near_lane)
    col_hot = (iota((lab_ref.shape[2], rows), 0) == column).astype(BF)
    labels = row_dot((dest_hot * label).astype(BF), col_hot)
    lane_hot = (iota((n_cent, rows), 0) == jnp.where(is_over, -1, toward)).astype(F32)
    lane_before = jnp.dot(lane_hot.astype(BF), upper, preferred_element_type=F32)
    packed = jnp.sum(lane_hot * lane_before, axis=0, keepdims=True).astype(jnp.int32)
    limit = send_ref.shape[1]
    crowded = jnp.sum(
        jnp.where((packed >= limit) & jnp.logical_not(is_over), 1.0, 0.0), axis=1, keepdims=True
    ) > 0.0
    lab_ref[:, 0, :] = labels + jnp.where(excess | crowded, SPILL, 0.0)
    seat_hot = (iota((index_ref.shape[2], rows), 0) == packed).astype(BF)
    index_ref[:, 0, :] = row_dot((lane_hot * (near_lane + 1).astype(F32)).astype(BF), seat_hot)
    meta_ref[...] = jnp.where(iota((8, rows), 0) == 0, dest, column)
    emb = emb_ref[...]
    unit = (emb * lax.rsqrt(jnp.sum(emb * emb, axis=1, keepdims=True) + EPSILON)).astype(BF)
    seat = jnp.where(is_over, -1, jnp.where(packed < limit, toward * limit + packed, -1))
    for c in range(n_cent):
        hot = (iota((limit, rows), 0) + c * limit == seat).astype(BF)
        send_ref[c] = jnp.dot(hot, unit, preferred_element_type=F32).astype(BF)
    pool_hot = (iota((pool, rows), 0) == jnp.where(is_over, pool_at, -1)).astype(BF)
    pool_ref[...] = jnp.dot(pool_hot, unit, preferred_element_type=F32).astype(BF)


def who(n_cent, index):
    return (index // n_cent, index % n_cent)


def enter(n_samp, n_cent, me):
    devices = n_samp * n_cent
    barrier = pltpu.get_barrier_semaphore()

    def greet(k, _):
        pl.semaphore_signal(
            barrier, inc=1, device_id=who(n_cent, (me + k) % devices), device_id_type=MESH
        )
        return 0

    lax.fori_loop(1, devices, greet, 0)
    pl.semaphore_wait(barrier, devices - 1)


def dedup_kernel(
    n_samp, n_cent, send_ref, pool_ref, index_ref, lab_ref, cent_ref, rep_ref, back_ref, tags_ref,
    lane_ref, seat_ref, stage_ref, near_ref, pools_ref, labs_ref, x_ref, col_ref, turn_ref, dens_ref,
    sums_ref, out_ref,
    own_sem, row_out, row_in, lab_out, lab_in, near_out, near_in, far_out, far_in, back_out, back_in,
    lane_out, lane_in, seat_out, seat_in, fwd_out,
):
    samp = lax.axis_index("samp")
    cent = lax.axis_index("cent")
    me = samp * n_cent + cent
    per_owner = cent_ref.shape[0]
    near = near_ref.shape[2]
    pool = pools_ref.shape[2]
    width = x_ref.shape[1]
    limit = lane_ref.shape[1]
    span = n_samp * near
    block = span
    quads = n_samp // 2
    count = n_cent + quads
    evens = list(range(0, n_samp, 2))

    def loop(low, high, body):
        def step(k, _):
            body(k)
            return 0
        lax.fori_loop(low, high, step, 0)

    def target(shift, c):
        return ((samp + shift) % n_samp, c)

    def near_copy(c, slot):
        return pltpu.make_async_remote_copy(
            pool_ref, pools_ref.at[0, slot], near_out.at[c], near_in.at[slot],
            device_id=(samp, c), device_id_type=MESH,
        )

    def lane_copy(c, slot):
        return pltpu.make_async_remote_copy(
            send_ref.at[c], lane_ref.at[slot], lane_out.at[c], lane_in.at[slot],
            device_id=(samp, c), device_id_type=MESH,
        )

    def seat_copy(c, slot):
        return pltpu.make_async_remote_copy(
            index_ref.at[c], seat_ref.at[slot], seat_out.at[c], seat_in.at[slot],
            device_id=(samp, c), device_id_type=MESH,
        )

    def row_copy(k, c):
        return pltpu.make_async_remote_copy(
            stage_ref.at[c, k], near_ref.at[c, k], row_out.at[k, c], row_in.at[k, c],
            device_id=target(k, cent), device_id_type=MESH,
        )

    def lab_copy(k, c, slot):
        s, t = target(k, c)
        return pltpu.make_async_remote_copy(
            lab_ref.at[s * n_cent + t], labs_ref.at[k, slot], lab_out.at[k, c], lab_in.at[k, slot],
            device_id=(s, t), device_id_type=MESH,
        )

    def far_copy(k):
        return pltpu.make_async_remote_copy(
            pools_ref.at[0], pools_ref.at[k], far_out.at[k], far_in.at[k],
            device_id=target(k, cent), device_id_type=MESH,
        )

    turn_by = 1 + (n_samp - 2) * (samp % 2)

    def forward(k):
        slot = (k + turn_by) % n_samp
        return pltpu.make_async_remote_copy(
            pools_ref.at[k], pools_ref.at[slot], fwd_out.at[k], far_in.at[slot],
            device_id=target(turn_by, cent), device_id_type=MESH,
        )

    def back_copy(k, c, slot, at_c):
        s = (samp + n_samp - k) % n_samp
        return pltpu.make_async_remote_copy(
            out_ref.at[c, samp_pair(k)], back_ref.at[slot], back_out.at[k, c], back_in.at[k, at_c],
            device_id=(s, c), device_id_type=MESH,
        )

    def samp_pair(k):
        return (k // 4) + (k % 2) * (n_samp // 4)

    def others(k, body):
        loop(1 if k == 0 else 0, n_cent, lambda c: body((cent + c) % n_cent))

    own = [
        pltpu.make_async_copy(send_ref.at[cent], lane_ref.at[cent], own_sem.at[0]),
        pltpu.make_async_copy(lab_ref.at[me], labs_ref.at[0, cent], own_sem.at[1]),
        pltpu.make_async_copy(pool_ref, pools_ref.at[0, cent], own_sem.at[2]),
        pltpu.make_async_copy(index_ref.at[cent], seat_ref.at[cent], own_sem.at[3]),
    ]
    for copy in own:
        copy.start()
    enter(n_samp, n_cent, me)
    others(0, lambda c: seat_copy(c, cent).start())
    others(0, lambda c: near_copy(c, cent).start())
    others(0, lambda c: lane_copy(c, cent).start())
    for k in range(n_samp):
        others(k, lambda c: lab_copy(k, c, cent).start())
    turn_ref[...] = jnp.zeros_like(turn_ref)
    sums_ref[...] = jnp.zeros_like(sums_ref)
    for copy in own:
        copy.wait()

    def spread(c):
        seat = seat_ref[c][:, 0:limit].astype(jnp.int32)
        hot = (iota((span, limit), 0) + 1 == seat).astype(BF)
        rows = jnp.dot(hot, lane_ref[c], preferred_element_type=F32).astype(BF)
        stage_ref[c] = rows.reshape(n_samp, near, width)

    def pass_on(c):
        loop(1, n_samp, lambda k: row_copy(k, c).start())

    spread(cent)
    others(0, lambda c: near_copy(c, c).wait_recv())
    pass_on(cent)
    for k in evens[1:]:
        far_copy(k).start()
    forward(0).start()
    for k in range(n_samp):
        others(k, lambda c: lab_copy(k, c, c).wait_recv())

    def score(p, load, tag):
        at = p * block
        load(at)
        tags_ref[p] = tag
        for start in range(0, block, LANES):
            chunk = jnp.broadcast_to(tag[:, start:start + LANES], (LANES, LANES))
            col_ref[at + start:at + start + LANES, :] = jnp.transpose(chunk)
        fresh = x_ref[at:at + block, :]
        member = (tag == (iota((per_owner, block), 0) + 1).astype(F32)).astype(BF)
        sums_ref[...] += jnp.dot(member, fresh, preferred_element_type=F32)

        def piece(top, height):
            gram = row_dot(x_ref[pl.ds(top, height), :], fresh)
            left = col_ref[pl.ds(top, height), :]
            same = jnp.concatenate([left] * (block // LANES), axis=1) == tag
            return jnp.where(same, jnp.exp(SHARPNESS * (gram - 1.0)), 0.0)

        def both(top, height):
            part = piece(top, height)
            folded = part[:, 0:LANES]
            for start in range(LANES, block, LANES):
                folded = folded + part[:, start:start + LANES]
            turn_ref[pl.ds(top, height), :] += folded
            return jnp.sum(part, axis=0, keepdims=True)

        total = jnp.sum(piece(at, block), axis=0, keepdims=True)
        if p >= 2:
            total = lax.fori_loop(
                0, p // 2,
                lambda j, t: t + both(pl.multiple_of(j * 2 * block, 2 * block), 2 * block),
                total,
            )
        if p % 2:
            total = total + both((p - 1) * block, block)
        dens_ref[p] = total

    def near_block(p, i):
        c = (cent + i) % n_cent
        tag = labs_ref[0, c][:, 0:span]
        for k in range(1, n_samp):
            tag = tag + labs_ref[k, c][:, 0:span]
        loop(1, n_samp, lambda k: row_copy(k, c).wait_recv())

        def load(at):
            x_ref[at:at + near, :] = stage_ref[c, 0]
            x_ref[at + near:at + block, :] = near_ref[c, 1:].reshape(block - near, width)

        score(p, load, tag)

    def pool_block(p, q):
        first = 4 * (q % (n_samp // 4)) + q // (n_samp // 4)
        half = n_cent * pool
        tag = jnp.zeros((1, block), F32)
        for k in (first, first + 2):
            for c in range(n_cent):
                tag = tag + labs_ref[k, c][:, span:span + block]
            if k > 0:
                far_copy(k).wait_recv()
                if k % 2 == 0:
                    forward(k).start()

        def load(at):
            x_ref[at:at + half, :] = pools_ref[first].reshape(half, width)
            x_ref[at + half:at + block, :] = pools_ref[first + 2].reshape(half, width)

        score(p, load, tag)

    for i in range(1, n_cent):
        c = (cent + i) % n_cent
        seat_copy(c, c).wait_recv()
        lane_copy(c, c).wait_recv()
        spread(c)
        pass_on(c)
    order = [(True, 0)] + [(False, q) for q in range(quads // 2)]
    order += [(True, i) for i in range(1, n_cent)]
    order += [(False, q) for q in range(quads // 2, quads)]
    for p, (is_near, which) in enumerate(order):
        if is_near:
            near_block(p, which)
        else:
            pool_block(p, which)

    sums = sums_ref[...]
    scale = lax.rsqrt(jnp.sum(sums * sums, axis=1, keepdims=True) + EPSILON)
    centroid = sums * scale
    cent_ref[...] = centroid
    high = centroid.astype(BF)
    low = (centroid - high.astype(F32)).astype(BF)
    pair = jnp.concatenate([high, low], axis=0)
    for p in range(count):
        at = p * block
        tag = tags_ref[p]
        valid = tag > 0.0
        member = tag == (iota((per_owner, block), 0) + 1).astype(F32)
        towards = row_dot(pair, x_ref[at:at + block, :])
        towards = towards[0:per_owner, :] + towards[per_owner:, :]
        similar = jnp.sum(jnp.where(member, towards, 0.0), axis=0, keepdims=True)
        flipped = []
        for start in range(at, at + block, LANES):
            flipped.append(
                jnp.sum(jnp.transpose(turn_ref[start:start + LANES, :]), axis=0, keepdims=True)
            )
        density = jnp.where(valid, dens_ref[p] + jnp.concatenate(flipped, axis=1), 1.0)
        weight = jnp.where(valid, jnp.exp(1.0 - similar) / density, 0.0)
        dens_ref[p] = weight
        is_near, which = order[p]
        if is_near:
            c = (cent + which) % n_cent
            for q in range(quads):
                out_ref[c, q, :, 0:span] = weight
        else:
            for c in range(n_cent):
                out_ref[c, which, :, span:span + block] = weight
    mine = pltpu.make_async_copy(out_ref.at[cent, 0], back_ref.at[me], own_sem.at[4])
    mine.start()
    mine.wait()
    for k in range(n_samp):
        others(k, lambda c: back_copy(k, c, me, cent).start())
    mixed = jnp.zeros(sums_ref.shape, F32)
    for p in range(count):
        member = tags_ref[p] == (iota((per_owner, block), 0) + 1).astype(F32)
        mixed = mixed + jnp.dot(
            jnp.where(member, dens_ref[p], 0.0).astype(BF), x_ref[p * block:(p + 1) * block, :],
            preferred_element_type=F32,
        )
    rep_ref[...] = mixed * lax.rsqrt(jnp.sum(mixed * mixed, axis=1, keepdims=True) + EPSILON)
    others(0, lambda c: seat_copy(c, cent).wait_send())
    others(0, lambda c: near_copy(c, cent).wait_send())
    others(0, lambda c: lane_copy(c, cent).wait_send())
    loop(0, n_cent, lambda c: loop(1, n_samp, lambda k: row_copy(k, c).wait_send()))
    for k in range(n_samp):
        others(k, lambda c: lab_copy(k, c, cent).wait_send())
        if k % 2 == 0:
            forward(k).wait_send()
            if k > 0:
                far_copy(k).wait_send()
        others(k, lambda c: back_copy(k, c, me, cent).wait_send())
    for k in range(n_samp):
        others(k, lambda c: back_copy(k, c, ((samp + k) % n_samp) * n_cent + c, c).wait_recv())


def pick_kernel(back_ref, meta_ref, keep_ref):
    devices = back_ref.shape[0]
    rows = meta_ref.shape[1]
    meta = meta_ref[...]
    dest_hot = (iota((devices, rows), 0) == meta[0:1, :]).astype(F32)
    spread = lax.dot_general(
        back_ref[:, 0, :], dest_hot, (((0,), (0,)), ((), ())),
        preferred_element_type=F32, precision=lax.Precision.HIGHEST,
    )
    hit = iota((back_ref.shape[2], rows), 0) == meta[1:2, :]
    keep_ref[...] = jnp.sum(jnp.where(hit, spread, 0.0), axis=0, keepdims=True)


def all_pairs(arrived, arrived_tags, validity, block_size):
    slot_count, feature_width = arrived.shape
    block_count = slot_count // block_size

    def score_block(pieces):
        block_rows, block_tags = pieces
        gram = jnp.einsum("rd,qd->rq", block_rows, arrived, preferred_element_type=jnp.float32)
        same_cluster = (block_tags[:, None] == arrived_tags[None, :]) & validity[None, :]
        similar = jnp.sum(jnp.where(same_cluster, gram, 0.0), axis=1)
        density = jnp.sum(jnp.where(same_cluster, jnp.exp(SHARPNESS * (gram - 1.0)), 0.0), axis=1)
        return (similar, density)

    similar, density = lax.map(
        score_block,
        (
            arrived.reshape(block_count, block_size, feature_width),
            arrived_tags.reshape(block_count, block_size),
        ),
    )
    return (similar.reshape(slot_count), density.reshape(slot_count))


def full_capacity(embeddings, assignment, owner_map):
    row_count, feature_width = embeddings.shape
    devices = lax.axis_size("samp") * lax.axis_size("cent")
    clusters = owner_map.shape[0]
    per_owner = clusters // devices
    capacity = 4 * row_count // devices
    slot_count = devices * capacity
    unit_rows = (
        embeddings * lax.rsqrt(jnp.sum(embeddings * embeddings, axis=1, keepdims=True) + EPSILON)
    ).astype(jnp.bfloat16)
    destination = owner_map[assignment]
    cluster_order = jnp.argsort(owner_map, stable=True)
    position = (
        jnp.zeros((clusters,), jnp.int32)
        .at[cluster_order]
        .set(jnp.arange(clusters, dtype=jnp.int32))
    )
    local_rank = position[assignment] - destination * per_owner
    dest_onehot = (destination[:, None] == jnp.arange(devices, dtype=jnp.int32)[None, :]).astype(
        jnp.int32
    )
    within_rank = jnp.sum(jnp.cumsum(dest_onehot, axis=0) * dest_onehot, axis=1) - 1
    slot_index = destination * capacity + within_rank
    outgoing = jnp.zeros((slot_count, feature_width), jnp.bfloat16).at[slot_index].set(unit_rows)
    labels = (
        jnp.zeros((slot_count,), jnp.bfloat16)
        .at[slot_index]
        .set((local_rank + 1).astype(jnp.bfloat16))
    )
    arrived, arrived_labels = (
        lax.all_to_all(outgoing, ("samp", "cent"), split_axis=0, concat_axis=0, tiled=True),
        lax.all_to_all(labels, ("samp", "cent"), split_axis=0, concat_axis=0, tiled=True),
    )
    arrived_tags = arrived_labels.astype(jnp.int32) - 1
    validity = arrived_tags >= 0
    block_size = min(512, slot_count)
    similar, density = all_pairs(arrived, arrived_tags, validity, block_size)
    member = arrived_tags[None, :] == jnp.arange(per_owner, dtype=jnp.int32)[:, None]
    member_bf = member.astype(jnp.bfloat16)
    cluster_sums = jnp.dot(member_bf, arrived, preferred_element_type=jnp.float32)
    inverse_norm = lax.rsqrt(jnp.sum(cluster_sums * cluster_sums, axis=1) + EPSILON)
    row_scale = jnp.sum(member.astype(jnp.float32) * inverse_norm[:, None], axis=0)
    spread = 1.0 - similar * row_scale
    weight = jnp.where(validity, jnp.exp(spread) / jnp.where(validity, density, 1.0), 0.0)
    weighted = jnp.dot(
        member_bf * weight.astype(jnp.bfloat16)[None, :],
        arrived,
        preferred_element_type=jnp.float32,
    )
    centroid = cluster_sums * inverse_norm[:, None]
    representative = weighted * lax.rsqrt(
        jnp.sum(weighted * weighted, axis=1, keepdims=True) + EPSILON
    )
    returned = lax.all_to_all(weight, ("samp", "cent"), split_axis=0, concat_axis=0, tiled=True)
    keep_weight = returned[slot_index]
    return (centroid, representative, keep_weight)


def on_device(embeddings, assignment, owner_map):
    rows, width = embeddings.shape
    n_samp = lax.axis_size("samp")
    n_cent = lax.axis_size("cent")
    devices = n_samp * n_cent
    clusters = owner_map.shape[0]
    per_owner = clusters // devices
    capacity = 4 * rows // devices
    near = capacity // 2
    pool = capacity - near
    vmem = pl.BlockSpec(memory_space=pltpu.VMEM)
    anywhere = pl.BlockSpec(memory_space=pl.ANY)
    shape = jax.ShapeDtypeStruct
    dma = pltpu.SemaphoreType.DMA
    block = n_samp * near
    blocks = n_cent + n_samp // 2
    slots = blocks * block
    limit = 21 * block // 32 // 8 * 8
    room = (limit + LANES - 1) // LANES * LANES
    send, pooled, index, labels, meta = pl.pallas_call(
        functools.partial(pack_kernel, devices, n_cent, near, pool),
        out_shape=(
            shape((n_cent, limit, width), BF),
            shape((pool, width), BF),
            shape((n_cent, 1, room), F32),
            shape((devices, 1, 2 * block), F32),
            shape((8, rows), jnp.int32),
        ),
        in_specs=[vmem] * 3,
        out_specs=(vmem,) * 5,
        name="pack",
    )(embeddings, assignment.reshape(1, rows), owner_map.reshape(1, clusters))
    centroid, representative, back, tags = pl.pallas_call(
        functools.partial(dedup_kernel, n_samp, n_cent),
        out_shape=(
            shape((per_owner, width), F32),
            shape((per_owner, width), F32),
            shape((devices, 1, 2 * block), F32),
            shape((blocks, 1, block), F32),
        ),
        in_specs=[anywhere] * 4,
        out_specs=(vmem,) * 4,
        scratch_shapes=[
            pltpu.VMEM((n_cent, limit, width), BF),
            pltpu.VMEM((n_cent, 1, room), F32),
            pltpu.VMEM((n_cent, n_samp, near, width), BF),
            pltpu.VMEM((n_cent, n_samp, near, width), BF),
            pltpu.VMEM((n_samp, n_cent, pool, width), BF),
            pltpu.VMEM((n_samp, n_cent, 1, 2 * block), F32),
            pltpu.VMEM((slots, width), BF),
            pltpu.VMEM((slots, LANES), F32),
            pltpu.VMEM((slots, LANES), F32),
            pltpu.VMEM((blocks, 1, block), F32),
            pltpu.VMEM((per_owner, width), F32),
            pltpu.VMEM((n_cent, n_samp // 2, 1, 2 * block), F32),
            dma((5,)),
            dma((n_samp, n_cent)), dma((n_samp, n_cent)), dma((n_samp, n_cent)), dma((n_samp, n_cent)),
            dma((n_cent,)), dma((n_cent,)), dma((n_samp,)), dma((n_samp,)),
            dma((n_samp, n_cent)), dma((n_samp, n_cent)),
            dma((n_cent,)), dma((n_cent,)), dma((n_cent,)), dma((n_cent,)), dma((n_samp,)),
        ],
        compiler_params=pltpu.CompilerParams(collective_id=0, has_side_effects=True),
        name="dedup",
    )(send, pooled, index, labels)
    keep = pl.pallas_call(
        pick_kernel,
        out_shape=shape((1, rows), F32),
        in_specs=[vmem] * 2,
        out_specs=vmem,
        name="pick",
    )(back, meta).reshape(rows)

    def fast(embeddings, assignment, owner_map, centroid, representative, keep):
        return centroid, representative, keep

    def slow(embeddings, assignment, owner_map, centroid, representative, keep):
        return full_capacity(embeddings, assignment, owner_map)

    spilled = jnp.max(tags) >= SPILL
    return lax.cond(
        spilled, slow, fast, embeddings, assignment, owner_map, centroid, representative, keep
    )


def solution(mesh):
    in_specs = (P(("samp", "cent"), None), P(("samp", "cent")), P())
    out_specs = (P(("samp", "cent"), None), P(("samp", "cent"), None), P(("samp", "cent")))
    return jax.shard_map(
        on_device, mesh=mesh, in_specs=in_specs, out_specs=out_specs, check_vma=False
    )
```

```python
import functools

import jax
import jax.numpy as jnp
from jax import lax
from jax.experimental import pallas as pl
from jax.experimental.pallas import tpu as pltpu
from jax.sharding import PartitionSpec as P

EPSILON = 1e-06
SHARPNESS = 8.0
LANES = 128
SPILL = 65536.0
BF = jnp.bfloat16
F32 = jnp.float32
MESH = pl.DeviceIdType.MESH


def iota(shape, axis):
    return lax.broadcasted_iota(jnp.int32, shape, axis)


def row_dot(a, b):
    return lax.dot_general(a, b, (((1,), (1,)), ((), ())), preferred_element_type=F32)


def samp_half(shift):
    return (shift // 2) % 2


def pack_kernel(devices, n_cent, near, pool, emb_ref, assign_ref, owner_ref, send_ref, pool_ref, index_ref, lab_ref, meta_ref):
    rows = emb_ref.shape[0]
    clusters = owner_ref.shape[1]
    upper = (iota((rows, rows), 0) < iota((rows, rows), 1)).astype(BF)
    owner = owner_ref[...]
    owner_hot = (iota((devices, clusters), 0) == owner).astype(F32)
    base = jnp.zeros((devices, 1), F32)
    ranks = []
    for start in range(0, clusters, rows):
        part = owner_hot[:, start:start + rows]
        before = jnp.dot(part.astype(BF), upper, preferred_element_type=F32) + base
        ranks.append(jnp.sum(part * before, axis=0, keepdims=True))
        base = base + jnp.sum(part, axis=1, keepdims=True)
    rank = jnp.concatenate(ranks, axis=1)
    assign = assign_ref[...]
    pick = (iota((clusters, rows), 0) == assign).astype(BF)
    which = iota((8, clusters), 0)
    table = jnp.where(which == 0, owner.astype(F32), jnp.where(which == 1, rank, 0.0)).astype(BF)
    found = jnp.dot(table, pick, preferred_element_type=F32)
    dest = found[0:1, :].astype(jnp.int32)
    label = found[1:2, :] + 1.0
    dest_hot = (iota((devices, rows), 0) == dest).astype(F32)
    before = jnp.dot(dest_hot.astype(BF), upper, preferred_element_type=F32)
    within = jnp.sum(dest_hot * before, axis=0, keepdims=True)
    over = (within >= near).astype(F32)
    over_before = jnp.dot(
        jnp.broadcast_to(over, (8, rows)).astype(BF), upper, preferred_element_type=F32
    )[0:1, :]
    excess = jnp.sum(over, axis=1, keepdims=True) > pool
    within = within.astype(jnp.int32)
    is_over = over > 0.0
    pool_at = over_before.astype(jnp.int32)
    samp = lax.axis_index("samp")
    cent = lax.axis_index("cent")
    n_samp = devices // n_cent
    span = n_samp * near
    shift = (dest // n_cent + n_samp - samp) % n_samp
    toward = dest % n_cent
    near_lane = shift * near + within
    pair_lane = (samp_half(shift) * n_cent + cent) * pool + jnp.minimum(pool_at, pool - 1)
    column = jnp.where(is_over, span + pair_lane, near_lane)
    col_hot = (iota((lab_ref.shape[2], rows), 0) == column).astype(BF)
    labels = row_dot((dest_hot * label).astype(BF), col_hot)
    lane_hot = (iota((n_cent, rows), 0) == jnp.where(is_over, -1, toward)).astype(F32)
    lane_before = jnp.dot(lane_hot.astype(BF), upper, preferred_element_type=F32)
    packed = jnp.sum(lane_hot * lane_before, axis=0, keepdims=True).astype(jnp.int32)
    limit = send_ref.shape[1]
    crowded = jnp.sum(
        jnp.where((packed >= limit) & jnp.logical_not(is_over), 1.0, 0.0), axis=1, keepdims=True
    ) > 0.0
    lab_ref[:, 0, :] = labels + jnp.where(excess | crowded, SPILL, 0.0)
    seat_hot = (iota((index_ref.shape[2], rows), 0) == packed).astype(BF)
    index_ref[:, 0, :] = row_dot((lane_hot * (near_lane + 1).astype(F32)).astype(BF), seat_hot)
    meta_ref[...] = jnp.where(iota((8, rows), 0) == 0, dest, column)
    emb = emb_ref[...]
    unit = (emb * lax.rsqrt(jnp.sum(emb * emb, axis=1, keepdims=True) + EPSILON)).astype(BF)
    seat = jnp.where(is_over, -1, jnp.where(packed < limit, toward * limit + packed, -1))
    for c in range(n_cent):
        hot = (iota((limit, rows), 0) + c * limit == seat).astype(BF)
        send_ref[c] = jnp.dot(hot, unit, preferred_element_type=F32).astype(BF)
    pool_hot = (iota((pool, rows), 0) == jnp.where(is_over, pool_at, -1)).astype(BF)
    pool_ref[...] = jnp.dot(pool_hot, unit, preferred_element_type=F32).astype(BF)


def who(n_cent, index):
    return (index // n_cent, index % n_cent)


def enter(n_samp, n_cent, me):
    devices = n_samp * n_cent
    barrier = pltpu.get_barrier_semaphore()

    def greet(k, _):
        pl.semaphore_signal(
            barrier, inc=1, device_id=who(n_cent, (me + k) % devices), device_id_type=MESH
        )
        return 0

    lax.fori_loop(1, devices, greet, 0)
    pl.semaphore_wait(barrier, devices - 1)


def dedup_kernel(
    n_samp, n_cent, send_ref, pool_ref, index_ref, lab_ref, cent_ref, rep_ref, back_ref, tags_ref,
    lane_ref, seat_ref, stage_ref, near_ref, pools_ref, labs_ref, x_ref, col_ref, turn_ref, dens_ref,
    sums_ref, out_ref,
    own_sem, row_out, row_in, lab_out, lab_in, near_out, near_in, far_out, far_in, back_out, back_in,
    lane_out, lane_in, seat_out, seat_in, fwd_out,
):
    samp = lax.axis_index("samp")
    cent = lax.axis_index("cent")
    me = samp * n_cent + cent
    per_owner = cent_ref.shape[0]
    near = near_ref.shape[2]
    pool = pools_ref.shape[2]
    width = x_ref.shape[1]
    limit = lane_ref.shape[1]
    span = n_samp * near
    block = span
    quads = n_samp // 2
    count = n_cent + quads
    evens = list(range(0, n_samp, 2))

    def loop(low, high, body):
        def step(k, _):
            body(k)
            return 0
        lax.fori_loop(low, high, step, 0)

    def target(shift, c):
        return ((samp + shift) % n_samp, c)

    def near_copy(c, slot):
        return pltpu.make_async_remote_copy(
            pool_ref, pools_ref.at[0, slot], near_out.at[c], near_in.at[slot],
            device_id=(samp, c), device_id_type=MESH,
        )

    def lane_copy(c, slot):
        return pltpu.make_async_remote_copy(
            send_ref.at[c], lane_ref.at[slot], lane_out.at[c], lane_in.at[slot],
            device_id=(samp, c), device_id_type=MESH,
        )

    def seat_copy(c, slot):
        return pltpu.make_async_remote_copy(
            index_ref.at[c], seat_ref.at[slot], seat_out.at[c], seat_in.at[slot],
            device_id=(samp, c), device_id_type=MESH,
        )

    def row_copy(k, c):
        return pltpu.make_async_remote_copy(
            stage_ref.at[c, k], near_ref.at[c, k], row_out.at[k, c], row_in.at[k, c],
            device_id=target(k, cent), device_id_type=MESH,
        )

    def lab_copy(k, c, slot):
        s, t = target(k, c)
        return pltpu.make_async_remote_copy(
            lab_ref.at[s * n_cent + t], labs_ref.at[k, slot], lab_out.at[k, c], lab_in.at[k, slot],
            device_id=(s, t), device_id_type=MESH,
        )

    def far_copy(k):
        return pltpu.make_async_remote_copy(
            pools_ref.at[0], pools_ref.at[k], far_out.at[k], far_in.at[k],
            device_id=target(k, cent), device_id_type=MESH,
        )

    turn_by = 1 + (n_samp - 2) * (samp % 2)

    def forward(k):
        slot = (k + turn_by) % n_samp
        return pltpu.make_async_remote_copy(
            pools_ref.at[k], pools_ref.at[slot], fwd_out.at[k], far_in.at[slot],
            device_id=target(turn_by, cent), device_id_type=MESH,
        )

    def back_copy(k, c, slot, at_c):
        s = (samp + n_samp - k) % n_samp
        return pltpu.make_async_remote_copy(
            out_ref.at[c, samp_pair(k)], back_ref.at[slot], back_out.at[k, c], back_in.at[k, at_c],
            device_id=(s, c), device_id_type=MESH,
        )

    def samp_pair(k):
        return (k // 4) + (k % 2) * (n_samp // 4)

    def others(k, body):
        loop(1 if k == 0 else 0, n_cent, lambda c: body((cent + c) % n_cent))

    own = [
        pltpu.make_async_copy(send_ref.at[cent], lane_ref.at[cent], own_sem.at[0]),
        pltpu.make_async_copy(lab_ref.at[me], labs_ref.at[0, cent], own_sem.at[1]),
        pltpu.make_async_copy(pool_ref, pools_ref.at[0, cent], own_sem.at[2]),
        pltpu.make_async_copy(index_ref.at[cent], seat_ref.at[cent], own_sem.at[3]),
    ]
    for copy in own:
        copy.start()
    enter(n_samp, n_cent, me)
    others(0, lambda c: seat_copy(c, cent).start())
    others(0, lambda c: near_copy(c, cent).start())
    others(0, lambda c: lane_copy(c, cent).start())
    for k in range(n_samp):
        others(k, lambda c: lab_copy(k, c, cent).start())
    turn_ref[...] = jnp.zeros_like(turn_ref)
    sums_ref[...] = jnp.zeros_like(sums_ref)
    for copy in own:
        copy.wait()

    def spread(c):
        seat = seat_ref[c][:, 0:limit].astype(jnp.int32)
        hot = (iota((span, limit), 0) + 1 == seat).astype(BF)
        rows = jnp.dot(hot, lane_ref[c], preferred_element_type=F32).astype(BF)
        stage_ref[c] = rows.reshape(n_samp, near, width)

    def pass_on(c):
        loop(1, n_samp, lambda k: row_copy(k, c).start())

    spread(cent)
    others(0, lambda c: near_copy(c, c).wait_recv())
    pass_on(cent)
    for k in evens[1:]:
        far_copy(k).start()
    forward(0).start()
    for k in range(n_samp):
        others(k, lambda c: lab_copy(k, c, c).wait_recv())

    def score(p, load, tag):
        at = p * block
        load(at)
        tags_ref[p] = tag
        for start in range(0, block, LANES):
            chunk = jnp.broadcast_to(tag[:, start:start + LANES], (LANES, LANES))
            col_ref[at + start:at + start + LANES, :] = jnp.transpose(chunk)
        fresh = x_ref[at:at + block, :]
        member = (tag == (iota((per_owner, block), 0) + 1).astype(F32)).astype(BF)
        sums_ref[...] += jnp.dot(member, fresh, preferred_element_type=F32)

        def piece(top, height):
            gram = row_dot(x_ref[pl.ds(top, height), :], fresh)
            left = col_ref[pl.ds(top, height), :]
            same = jnp.concatenate([left] * (block // LANES), axis=1) == tag
            return jnp.where(same, jnp.exp(SHARPNESS * (gram - 1.0)), 0.0)

        def both(top, height):
            part = piece(top, height)
            folded = part[:, 0:LANES]
            for start in range(LANES, block, LANES):
                folded = folded + part[:, start:start + LANES]
            turn_ref[pl.ds(top, height), :] += folded
            return jnp.sum(part, axis=0, keepdims=True)

        total = jnp.sum(piece(at, block), axis=0, keepdims=True)
        if p >= 2:
            total = lax.fori_loop(
                0, p // 2,
                lambda j, t: t + both(pl.multiple_of(j * 2 * block, 2 * block), 2 * block),
                total,
            )
        if p % 2:
            total = total + both((p - 1) * block, block)
        dens_ref[p] = total

    def near_block(p, i):
        c = (cent + i) % n_cent
        tag = labs_ref[0, c][:, 0:span]
        for k in range(1, n_samp):
            tag = tag + labs_ref[k, c][:, 0:span]
        loop(1, n_samp, lambda k: row_copy(k, c).wait_recv())

        def load(at):
            x_ref[at:at + near, :] = stage_ref[c, 0]
            x_ref[at + near:at + block, :] = near_ref[c, 1:].reshape(block - near, width)

        score(p, load, tag)

    def pool_block(p, q):
        first = 4 * (q % (n_samp // 4)) + q // (n_samp // 4)
        half = n_cent * pool
        tag = jnp.zeros((1, block), F32)
        for k in (first, first + 2):
            for c in range(n_cent):
                tag = tag + labs_ref[k, c][:, span:span + block]
            if k > 0:
                far_copy(k).wait_recv()
                if k % 2 == 0:
                    forward(k).start()

        def load(at):
            x_ref[at:at + half, :] = pools_ref[first].reshape(half, width)
            x_ref[at + half:at + block, :] = pools_ref[first + 2].reshape(half, width)

        score(p, load, tag)

    order = []

    def run(is_near, which):
        order.append((is_near, which))
        if is_near:
            near_block(len(order) - 1, which)
        else:
            pool_block(len(order) - 1, which)

    for i in range(1, n_cent):
        c = (cent + i) % n_cent
        seat_copy(c, c).wait_recv()
        lane_copy(c, c).wait_recv()
        spread(c)
        pass_on(c)
        if i == 1:
            run(True, 0)
        for q in range((i - 1) * quads // (n_cent - 1), i * quads // (n_cent - 1)):
            run(False, q)
    for i in range(1, n_cent):
        run(True, i)

    sums = sums_ref[...]
    scale = lax.rsqrt(jnp.sum(sums * sums, axis=1, keepdims=True) + EPSILON)
    centroid = sums * scale
    cent_ref[...] = centroid
    high = centroid.astype(BF)
    low = (centroid - high.astype(F32)).astype(BF)
    pair = jnp.concatenate([high, low], axis=0)
    for p in range(count):
        at = p * block
        tag = tags_ref[p]
        valid = tag > 0.0
        member = tag == (iota((per_owner, block), 0) + 1).astype(F32)
        towards = row_dot(pair, x_ref[at:at + block, :])
        towards = towards[0:per_owner, :] + towards[per_owner:, :]
        similar = jnp.sum(jnp.where(member, towards, 0.0), axis=0, keepdims=True)
        flipped = []
        for start in range(at, at + block, LANES):
            flipped.append(
                jnp.sum(jnp.transpose(turn_ref[start:start + LANES, :]), axis=0, keepdims=True)
            )
        density = jnp.where(valid, dens_ref[p] + jnp.concatenate(flipped, axis=1), 1.0)
        weight = jnp.where(valid, jnp.exp(1.0 - similar) / density, 0.0)
        dens_ref[p] = weight
        is_near, which = order[p]
        if is_near:
            c = (cent + which) % n_cent
            for q in range(quads):
                out_ref[c, q, :, 0:span] = weight
        else:
            for c in range(n_cent):
                out_ref[c, which, :, span:span + block] = weight
    mine = pltpu.make_async_copy(out_ref.at[cent, 0], back_ref.at[me], own_sem.at[4])
    mine.start()
    mine.wait()
    for k in range(n_samp):
        others(k, lambda c: back_copy(k, c, me, cent).start())
    mixed = jnp.zeros(sums_ref.shape, F32)
    for p in range(count):
        member = tags_ref[p] == (iota((per_owner, block), 0) + 1).astype(F32)
        mixed = mixed + jnp.dot(
            jnp.where(member, dens_ref[p], 0.0).astype(BF), x_ref[p * block:(p + 1) * block, :],
            preferred_element_type=F32,
        )
    rep_ref[...] = mixed * lax.rsqrt(jnp.sum(mixed * mixed, axis=1, keepdims=True) + EPSILON)
    others(0, lambda c: seat_copy(c, cent).wait_send())
    others(0, lambda c: near_copy(c, cent).wait_send())
    others(0, lambda c: lane_copy(c, cent).wait_send())
    loop(0, n_cent, lambda c: loop(1, n_samp, lambda k: row_copy(k, c).wait_send()))
    for k in range(n_samp):
        others(k, lambda c: lab_copy(k, c, cent).wait_send())
        if k % 2 == 0:
            forward(k).wait_send()
            if k > 0:
                far_copy(k).wait_send()
        others(k, lambda c: back_copy(k, c, me, cent).wait_send())
    for k in range(n_samp):
        others(k, lambda c: back_copy(k, c, ((samp + k) % n_samp) * n_cent + c, c).wait_recv())


def pick_kernel(back_ref, meta_ref, keep_ref):
    devices = back_ref.shape[0]
    rows = meta_ref.shape[1]
    meta = meta_ref[...]
    dest_hot = (iota((devices, rows), 0) == meta[0:1, :]).astype(F32)
    spread = lax.dot_general(
        back_ref[:, 0, :], dest_hot, (((0,), (0,)), ((), ())),
        preferred_element_type=F32, precision=lax.Precision.HIGHEST,
    )
    hit = iota((back_ref.shape[2], rows), 0) == meta[1:2, :]
    keep_ref[...] = jnp.sum(jnp.where(hit, spread, 0.0), axis=0, keepdims=True)


def all_pairs(arrived, arrived_tags, validity, block_size):
    slot_count, feature_width = arrived.shape
    block_count = slot_count // block_size

    def score_block(pieces):
        block_rows, block_tags = pieces
        gram = jnp.einsum("rd,qd->rq", block_rows, arrived, preferred_element_type=jnp.float32)
        same_cluster = (block_tags[:, None] == arrived_tags[None, :]) & validity[None, :]
        similar = jnp.sum(jnp.where(same_cluster, gram, 0.0), axis=1)
        density = jnp.sum(jnp.where(same_cluster, jnp.exp(SHARPNESS * (gram - 1.0)), 0.0), axis=1)
        return (similar, density)

    similar, density = lax.map(
        score_block,
        (
            arrived.reshape(block_count, block_size, feature_width),
            arrived_tags.reshape(block_count, block_size),
        ),
    )
    return (similar.reshape(slot_count), density.reshape(slot_count))


def full_capacity(embeddings, assignment, owner_map):
    row_count, feature_width = embeddings.shape
    devices = lax.axis_size("samp") * lax.axis_size("cent")
    clusters = owner_map.shape[0]
    per_owner = clusters // devices
    capacity = 4 * row_count // devices
    slot_count = devices * capacity
    unit_rows = (
        embeddings * lax.rsqrt(jnp.sum(embeddings * embeddings, axis=1, keepdims=True) + EPSILON)
    ).astype(jnp.bfloat16)
    destination = owner_map[assignment]
    cluster_order = jnp.argsort(owner_map, stable=True)
    position = (
        jnp.zeros((clusters,), jnp.int32)
        .at[cluster_order]
        .set(jnp.arange(clusters, dtype=jnp.int32))
    )
    local_rank = position[assignment] - destination * per_owner
    dest_onehot = (destination[:, None] == jnp.arange(devices, dtype=jnp.int32)[None, :]).astype(
        jnp.int32
    )
    within_rank = jnp.sum(jnp.cumsum(dest_onehot, axis=0) * dest_onehot, axis=1) - 1
    slot_index = destination * capacity + within_rank
    outgoing = jnp.zeros((slot_count, feature_width), jnp.bfloat16).at[slot_index].set(unit_rows)
    labels = (
        jnp.zeros((slot_count,), jnp.bfloat16)
        .at[slot_index]
        .set((local_rank + 1).astype(jnp.bfloat16))
    )
    arrived, arrived_labels = (
        lax.all_to_all(outgoing, ("samp", "cent"), split_axis=0, concat_axis=0, tiled=True),
        lax.all_to_all(labels, ("samp", "cent"), split_axis=0, concat_axis=0, tiled=True),
    )
    arrived_tags = arrived_labels.astype(jnp.int32) - 1
    validity = arrived_tags >= 0
    block_size = min(512, slot_count)
    similar, density = all_pairs(arrived, arrived_tags, validity, block_size)
    member = arrived_tags[None, :] == jnp.arange(per_owner, dtype=jnp.int32)[:, None]
    member_bf = member.astype(jnp.bfloat16)
    cluster_sums = jnp.dot(member_bf, arrived, preferred_element_type=jnp.float32)
    inverse_norm = lax.rsqrt(jnp.sum(cluster_sums * cluster_sums, axis=1) + EPSILON)
    row_scale = jnp.sum(member.astype(jnp.float32) * inverse_norm[:, None], axis=0)
    spread = 1.0 - similar * row_scale
    weight = jnp.where(validity, jnp.exp(spread) / jnp.where(validity, density, 1.0), 0.0)
    weighted = jnp.dot(
        member_bf * weight.astype(jnp.bfloat16)[None, :],
        arrived,
        preferred_element_type=jnp.float32,
    )
    centroid = cluster_sums * inverse_norm[:, None]
    representative = weighted * lax.rsqrt(
        jnp.sum(weighted * weighted, axis=1, keepdims=True) + EPSILON
    )
    returned = lax.all_to_all(weight, ("samp", "cent"), split_axis=0, concat_axis=0, tiled=True)
    keep_weight = returned[slot_index]
    return (centroid, representative, keep_weight)


def on_device(embeddings, assignment, owner_map):
    rows, width = embeddings.shape
    n_samp = lax.axis_size("samp")
    n_cent = lax.axis_size("cent")
    devices = n_samp * n_cent
    clusters = owner_map.shape[0]
    per_owner = clusters // devices
    capacity = 4 * rows // devices
    near = capacity // 2
    pool = capacity - near
    vmem = pl.BlockSpec(memory_space=pltpu.VMEM)
    anywhere = pl.BlockSpec(memory_space=pl.ANY)
    shape = jax.ShapeDtypeStruct
    dma = pltpu.SemaphoreType.DMA
    block = n_samp * near
    blocks = n_cent + n_samp // 2
    slots = blocks * block
    limit = 21 * block // 32 // 8 * 8
    room = (limit + LANES - 1) // LANES * LANES
    send, pooled, index, labels, meta = pl.pallas_call(
        functools.partial(pack_kernel, devices, n_cent, near, pool),
        out_shape=(
            shape((n_cent, limit, width), BF),
            shape((pool, width), BF),
            shape((n_cent, 1, room), F32),
            shape((devices, 1, 2 * block), F32),
            shape((8, rows), jnp.int32),
        ),
        in_specs=[vmem] * 3,
        out_specs=(vmem,) * 5,
        name="pack",
    )(embeddings, assignment.reshape(1, rows), owner_map.reshape(1, clusters))
    centroid, representative, back, tags = pl.pallas_call(
        functools.partial(dedup_kernel, n_samp, n_cent),
        out_shape=(
            shape((per_owner, width), F32),
            shape((per_owner, width), F32),
            shape((devices, 1, 2 * block), F32),
            shape((blocks, 1, block), F32),
        ),
        in_specs=[anywhere] * 4,
        out_specs=(vmem,) * 4,
        scratch_shapes=[
            pltpu.VMEM((n_cent, limit, width), BF),
            pltpu.VMEM((n_cent, 1, room), F32),
            pltpu.VMEM((n_cent, n_samp, near, width), BF),
            pltpu.VMEM((n_cent, n_samp, near, width), BF),
            pltpu.VMEM((n_samp, n_cent, pool, width), BF),
            pltpu.VMEM((n_samp, n_cent, 1, 2 * block), F32),
            pltpu.VMEM((slots, width), BF),
            pltpu.VMEM((slots, LANES), F32),
            pltpu.VMEM((slots, LANES), F32),
            pltpu.VMEM((blocks, 1, block), F32),
            pltpu.VMEM((per_owner, width), F32),
            pltpu.VMEM((n_cent, n_samp // 2, 1, 2 * block), F32),
            dma((5,)),
            dma((n_samp, n_cent)), dma((n_samp, n_cent)), dma((n_samp, n_cent)), dma((n_samp, n_cent)),
            dma((n_cent,)), dma((n_cent,)), dma((n_samp,)), dma((n_samp,)),
            dma((n_samp, n_cent)), dma((n_samp, n_cent)),
            dma((n_cent,)), dma((n_cent,)), dma((n_cent,)), dma((n_cent,)), dma((n_samp,)),
        ],
        compiler_params=pltpu.CompilerParams(collective_id=0, has_side_effects=True),
        name="dedup",
    )(send, pooled, index, labels)
    keep = pl.pallas_call(
        pick_kernel,
        out_shape=shape((1, rows), F32),
        in_specs=[vmem] * 2,
        out_specs=vmem,
        name="pick",
    )(back, meta).reshape(rows)

    def fast(embeddings, assignment, owner_map, centroid, representative, keep):
        return centroid, representative, keep

    def slow(embeddings, assignment, owner_map, centroid, representative, keep):
        return full_capacity(embeddings, assignment, owner_map)

    spilled = jnp.max(tags) >= SPILL
    return lax.cond(
        spilled, slow, fast, embeddings, assignment, owner_map, centroid, representative, keep
    )


def solution(mesh):
    in_specs = (P(("samp", "cent"), None), P(("samp", "cent")), P())
    out_specs = (P(("samp", "cent"), None), P(("samp", "cent"), None), P(("samp", "cent")))
    return jax.shard_map(
        on_device, mesh=mesh, in_specs=in_specs, out_specs=out_specs, check_vma=False
    )
```

```python
import functools

import jax
import jax.numpy as jnp
from jax import lax
from jax.experimental import pallas as pl
from jax.experimental.pallas import tpu as pltpu
from jax.sharding import PartitionSpec as P

EPSILON = 1e-06
SHARPNESS = 8.0
LANES = 128
SPILL = 65536.0
BF = jnp.bfloat16
F32 = jnp.float32
MESH = pl.DeviceIdType.MESH


def iota(shape, axis):
    return lax.broadcasted_iota(jnp.int32, shape, axis)


def row_dot(a, b):
    return lax.dot_general(a, b, (((1,), (1,)), ((), ())), preferred_element_type=F32)


def samp_half(shift):
    return (shift // 2) % 2


def pack_kernel(devices, n_cent, near, pool, emb_ref, assign_ref, owner_ref, send_ref, pool_ref, index_ref, lab_ref, meta_ref):
    rows = emb_ref.shape[0]
    clusters = owner_ref.shape[1]
    upper = (iota((rows, rows), 0) < iota((rows, rows), 1)).astype(BF)
    owner = owner_ref[...]
    owner_hot = (iota((devices, clusters), 0) == owner).astype(F32)
    base = jnp.zeros((devices, 1), F32)
    ranks = []
    for start in range(0, clusters, rows):
        part = owner_hot[:, start:start + rows]
        before = jnp.dot(part.astype(BF), upper, preferred_element_type=F32) + base
        ranks.append(jnp.sum(part * before, axis=0, keepdims=True))
        base = base + jnp.sum(part, axis=1, keepdims=True)
    rank = jnp.concatenate(ranks, axis=1)
    assign = assign_ref[...]
    pick = (iota((clusters, rows), 0) == assign).astype(BF)
    which = iota((8, clusters), 0)
    table = jnp.where(which == 0, owner.astype(F32), jnp.where(which == 1, rank, 0.0)).astype(BF)
    found = jnp.dot(table, pick, preferred_element_type=F32)
    dest = found[0:1, :].astype(jnp.int32)
    label = found[1:2, :] + 1.0
    dest_hot = (iota((devices, rows), 0) == dest).astype(F32)
    before = jnp.dot(dest_hot.astype(BF), upper, preferred_element_type=F32)
    within = jnp.sum(dest_hot * before, axis=0, keepdims=True)
    over = (within >= near).astype(F32)
    over_before = jnp.dot(
        jnp.broadcast_to(over, (8, rows)).astype(BF), upper, preferred_element_type=F32
    )[0:1, :]
    excess = jnp.sum(over, axis=1, keepdims=True) > pool
    within = within.astype(jnp.int32)
    is_over = over > 0.0
    pool_at = over_before.astype(jnp.int32)
    samp = lax.axis_index("samp")
    cent = lax.axis_index("cent")
    n_samp = devices // n_cent
    span = n_samp * near
    shift = (dest // n_cent + n_samp - samp) % n_samp
    toward = dest % n_cent
    near_lane = shift * near + within
    pair_lane = (samp_half(shift) * n_cent + cent) * pool + jnp.minimum(pool_at, pool - 1)
    column = jnp.where(is_over, span + pair_lane, near_lane)
    col_hot = (iota((lab_ref.shape[2], rows), 0) == column).astype(BF)
    labels = row_dot((dest_hot * label).astype(BF), col_hot)
    lane_hot = (iota((n_cent, rows), 0) == jnp.where(is_over, -1, toward)).astype(F32)
    lane_before = jnp.dot(lane_hot.astype(BF), upper, preferred_element_type=F32)
    packed = jnp.sum(lane_hot * lane_before, axis=0, keepdims=True).astype(jnp.int32)
    limit = send_ref.shape[1]
    crowded = jnp.sum(
        jnp.where((packed >= limit) & jnp.logical_not(is_over), 1.0, 0.0), axis=1, keepdims=True
    ) > 0.0
    lab_ref[:, 0, :] = labels + jnp.where(excess | crowded, SPILL, 0.0)
    seat_hot = (iota((index_ref.shape[2], rows), 0) == packed).astype(BF)
    index_ref[:, 0, :] = row_dot((lane_hot * (near_lane + 1).astype(F32)).astype(BF), seat_hot)
    meta_ref[...] = jnp.where(iota((8, rows), 0) == 0, dest, column)
    emb = emb_ref[...]
    unit = (emb * lax.rsqrt(jnp.sum(emb * emb, axis=1, keepdims=True) + EPSILON)).astype(BF)
    seat = jnp.where(is_over, -1, jnp.where(packed < limit, toward * limit + packed, -1))
    for c in range(n_cent):
        hot = (iota((limit, rows), 0) + c * limit == seat).astype(BF)
        send_ref[c] = jnp.dot(hot, unit, preferred_element_type=F32).astype(BF)
    pool_hot = (iota((pool, rows), 0) == jnp.where(is_over, pool_at, -1)).astype(BF)
    pool_ref[...] = jnp.dot(pool_hot, unit, preferred_element_type=F32).astype(BF)


def who(n_cent, index):
    return (index // n_cent, index % n_cent)


def enter(n_samp, n_cent, me):
    devices = n_samp * n_cent
    barrier = pltpu.get_barrier_semaphore()

    def greet(k, _):
        pl.semaphore_signal(
            barrier, inc=1, device_id=who(n_cent, (me + k) % devices), device_id_type=MESH
        )
        return 0

    lax.fori_loop(1, devices, greet, 0)
    pl.semaphore_wait(barrier, devices - 1)


def dedup_kernel(
    n_samp, n_cent, send_ref, pool_ref, index_ref, lab_ref, cent_ref, rep_ref, back_ref, tags_ref,
    lane_ref, seat_ref, stage_ref, near_ref, pools_ref, labs_ref, x_ref, col_ref, turn_ref, dens_ref,
    sums_ref, out_ref,
    own_sem, row_out, row_in, lab_out, lab_in, near_out, near_in, far_out, far_in, back_out, back_in,
    lane_out, lane_in, seat_out, seat_in, fwd_out,
):
    samp = lax.axis_index("samp")
    cent = lax.axis_index("cent")
    me = samp * n_cent + cent
    per_owner = cent_ref.shape[0]
    near = near_ref.shape[2]
    pool = pools_ref.shape[2]
    width = x_ref.shape[1]
    limit = lane_ref.shape[1]
    span = n_samp * near
    block = span
    quads = n_samp // 2
    count = n_cent + quads
    evens = list(range(0, n_samp, 2))

    def loop(low, high, body):
        def step(k, _):
            body(k)
            return 0
        lax.fori_loop(low, high, step, 0)

    def target(shift, c):
        return ((samp + shift) % n_samp, c)

    def near_copy(c, slot):
        return pltpu.make_async_remote_copy(
            pool_ref, pools_ref.at[0, slot], near_out.at[c], near_in.at[slot],
            device_id=(samp, c), device_id_type=MESH,
        )

    def lane_copy(c, slot):
        return pltpu.make_async_remote_copy(
            send_ref.at[c], lane_ref.at[slot], lane_out.at[c], lane_in.at[slot],
            device_id=(samp, c), device_id_type=MESH,
        )

    def seat_copy(c, slot):
        return pltpu.make_async_remote_copy(
            index_ref.at[c], seat_ref.at[slot], seat_out.at[c], seat_in.at[slot],
            device_id=(samp, c), device_id_type=MESH,
        )

    def row_copy(k, c):
        return pltpu.make_async_remote_copy(
            stage_ref.at[c, k], near_ref.at[c, k], row_out.at[k, c], row_in.at[k, c],
            device_id=target(k, cent), device_id_type=MESH,
        )

    def lab_copy(k, c, slot):
        s, t = target(k, c)
        return pltpu.make_async_remote_copy(
            lab_ref.at[s * n_cent + t], labs_ref.at[k, slot], lab_out.at[k, c], lab_in.at[k, slot],
            device_id=(s, t), device_id_type=MESH,
        )

    def far_copy(k):
        return pltpu.make_async_remote_copy(
            pools_ref.at[0], pools_ref.at[k], far_out.at[k], far_in.at[k],
            device_id=target(k, cent), device_id_type=MESH,
        )

    turn_by = 1 + (n_samp - 2) * (samp % 2)

    def forward(k):
        slot = (k + turn_by) % n_samp
        return pltpu.make_async_remote_copy(
            pools_ref.at[k], pools_ref.at[slot], fwd_out.at[k], far_in.at[slot],
            device_id=target(turn_by, cent), device_id_type=MESH,
        )

    def back_copy(k, c, slot, at_c):
        s = (samp + n_samp - k) % n_samp
        return pltpu.make_async_remote_copy(
            out_ref.at[c, samp_pair(k)], back_ref.at[slot], back_out.at[k, c], back_in.at[k, at_c],
            device_id=(s, c), device_id_type=MESH,
        )

    def samp_pair(k):
        return (k // 4) + (k % 2) * (n_samp // 4)

    def others(k, body):
        loop(1 if k == 0 else 0, n_cent, lambda c: body((cent + c) % n_cent))

    own = [
        pltpu.make_async_copy(send_ref.at[cent], lane_ref.at[cent], own_sem.at[0]),
        pltpu.make_async_copy(lab_ref.at[me], labs_ref.at[0, cent], own_sem.at[1]),
        pltpu.make_async_copy(pool_ref, pools_ref.at[0, cent], own_sem.at[2]),
        pltpu.make_async_copy(index_ref.at[cent], seat_ref.at[cent], own_sem.at[3]),
    ]
    for copy in own:
        copy.start()
    enter(n_samp, n_cent, me)
    others(0, lambda c: seat_copy(c, cent).start())
    others(0, lambda c: near_copy(c, cent).start())
    others(0, lambda c: lane_copy(c, cent).start())
    for k in range(n_samp):
        others(k, lambda c: lab_copy(k, c, cent).start())
    turn_ref[...] = jnp.zeros_like(turn_ref)
    sums_ref[...] = jnp.zeros_like(sums_ref)
    for copy in own:
        copy.wait()

    def spread(c):
        seat = seat_ref[c][:, 0:limit].astype(jnp.int32)
        hot = (iota((span, limit), 0) + 1 == seat).astype(BF)
        rows = jnp.dot(hot, lane_ref[c], preferred_element_type=F32).astype(BF)
        stage_ref[c] = rows.reshape(n_samp, near, width)

    def pass_on(c):
        loop(1, n_samp, lambda k: row_copy(k, c).start())

    spread(cent)
    others(0, lambda c: near_copy(c, c).wait_recv())
    pass_on(cent)
    for k in evens[1:]:
        far_copy(k).start()
    forward(0).start()
    for k in range(n_samp):
        others(k, lambda c: lab_copy(k, c, c).wait_recv())

    def score(p, load, tag):
        at = p * block
        load(at)
        tags_ref[p] = tag
        for start in range(0, block, LANES):
            chunk = jnp.broadcast_to(tag[:, start:start + LANES], (LANES, LANES))
            col_ref[at + start:at + start + LANES, :] = jnp.transpose(chunk)
        fresh = x_ref[at:at + block, :]
        member = (tag == (iota((per_owner, block), 0) + 1).astype(F32)).astype(BF)
        sums_ref[...] += jnp.dot(member, fresh, preferred_element_type=F32)

        def piece(top, height):
            gram = row_dot(x_ref[pl.ds(top, height), :], fresh)
            left = col_ref[pl.ds(top, height), :]
            same = jnp.concatenate([left] * (block // LANES), axis=1) == tag
            return jnp.where(same, jnp.exp(SHARPNESS * (gram - 1.0)), 0.0)

        def both(top, height):
            part = piece(top, height)
            folded = part[:, 0:LANES]
            for start in range(LANES, block, LANES):
                folded = folded + part[:, start:start + LANES]
            turn_ref[pl.ds(top, height), :] += folded
            return jnp.sum(part, axis=0, keepdims=True)

        total = jnp.sum(piece(at, block), axis=0, keepdims=True)
        if p >= 2:
            total = lax.fori_loop(
                0, p // 2,
                lambda j, t: t + both(pl.multiple_of(j * 2 * block, 2 * block), 2 * block),
                total,
            )
        if p % 2:
            total = total + both((p - 1) * block, block)
        dens_ref[p] = total

    def near_block(p, i):
        c = (cent + i) % n_cent
        tag = labs_ref[0, c][:, 0:span]
        for k in range(1, n_samp):
            tag = tag + labs_ref[k, c][:, 0:span]
        loop(1, n_samp, lambda k: row_copy(k, c).wait_recv())

        def load(at):
            x_ref[at:at + near, :] = stage_ref[c, 0]
            x_ref[at + near:at + block, :] = near_ref[c, 1:].reshape(block - near, width)

        score(p, load, tag)

    def pool_block(p, q):
        first = 4 * (q % (n_samp // 4)) + q // (n_samp // 4)
        half = n_cent * pool
        tag = jnp.zeros((1, block), F32)
        for k in (first, first + 2):
            for c in range(n_cent):
                tag = tag + labs_ref[k, c][:, span:span + block]
            if k > 0:
                far_copy(k).wait_recv()
                if k % 2 == 0:
                    forward(k).start()

        def load(at):
            x_ref[at:at + half, :] = pools_ref[first].reshape(half, width)
            x_ref[at + half:at + block, :] = pools_ref[first + 2].reshape(half, width)

        score(p, load, tag)

    order = []

    def run(is_near, which):
        order.append((is_near, which))
        if is_near:
            near_block(len(order) - 1, which)
        else:
            pool_block(len(order) - 1, which)

    for i in range(1, n_cent):
        c = (cent + i) % n_cent
        seat_copy(c, c).wait_recv()
        lane_copy(c, c).wait_recv()
        spread(c)
        pass_on(c)
        if i == 1:
            run(True, 0)
        for q in range((i - 1) * quads // (n_cent - 1), i * quads // (n_cent - 1)):
            run(False, q)
    for i in range(1, n_cent):
        run(True, i)

    sums = sums_ref[...]
    scale = lax.rsqrt(jnp.sum(sums * sums, axis=1, keepdims=True) + EPSILON)
    centroid = sums * scale
    cent_ref[...] = centroid
    high = centroid.astype(BF)
    low = (centroid - high.astype(F32)).astype(BF)
    pair = jnp.concatenate([high, low], axis=0)
    for p in range(count):
        at = p * block
        tag = tags_ref[p]
        valid = tag > 0.0
        member = tag == (iota((per_owner, block), 0) + 1).astype(F32)
        towards = row_dot(pair, x_ref[at:at + block, :])
        towards = towards[0:per_owner, :] + towards[per_owner:, :]
        similar = jnp.sum(jnp.where(member, towards, 0.0), axis=0, keepdims=True)
        flipped = []
        for start in range(at, at + block, LANES):
            flipped.append(
                jnp.sum(jnp.transpose(turn_ref[start:start + LANES, :]), axis=0, keepdims=True)
            )
        density = jnp.where(valid, dens_ref[p] + jnp.concatenate(flipped, axis=1), 1.0)
        weight = jnp.where(valid, jnp.exp(1.0 - similar) / density, 0.0)
        dens_ref[p] = weight
        is_near, which = order[p]
        if is_near:
            c = (cent + which) % n_cent
            for q in range(quads):
                out_ref[c, q, :, 0:span] = weight
        else:
            for c in range(n_cent):
                out_ref[c, which, :, span:span + block] = weight
    mine = pltpu.make_async_copy(out_ref.at[cent, 0], back_ref.at[me], own_sem.at[4])
    mine.start()
    mine.wait()
    for k in range(n_samp):
        others(k, lambda c: back_copy(k, c, me, cent).start())
    mixed = jnp.zeros(sums_ref.shape, F32)
    for p in range(count):
        member = tags_ref[p] == (iota((per_owner, block), 0) + 1).astype(F32)
        mixed = mixed + jnp.dot(
            jnp.where(member, dens_ref[p], 0.0).astype(BF), x_ref[p * block:(p + 1) * block, :],
            preferred_element_type=F32,
        )
    rep_ref[...] = mixed * lax.rsqrt(jnp.sum(mixed * mixed, axis=1, keepdims=True) + EPSILON)
    others(0, lambda c: seat_copy(c, cent).wait_send())
    others(0, lambda c: near_copy(c, cent).wait_send())
    others(0, lambda c: lane_copy(c, cent).wait_send())
    loop(0, n_cent, lambda c: loop(1, n_samp, lambda k: row_copy(k, c).wait_send()))
    for k in range(n_samp):
        others(k, lambda c: lab_copy(k, c, cent).wait_send())
        if k % 2 == 0:
            forward(k).wait_send()
            if k > 0:
                far_copy(k).wait_send()
        others(k, lambda c: back_copy(k, c, me, cent).wait_send())
    for k in range(n_samp):
        others(k, lambda c: back_copy(k, c, ((samp + k) % n_samp) * n_cent + c, c).wait_recv())


def pick_kernel(back_ref, meta_ref, tags_ref, keep_ref, top_ref):
    top_ref[0, 0] = jnp.max(tags_ref[:, 0, :])
    devices = back_ref.shape[0]
    rows = meta_ref.shape[1]
    meta = meta_ref[...]
    dest_hot = (iota((devices, rows), 0) == meta[0:1, :]).astype(F32)
    spread = lax.dot_general(
        back_ref[:, 0, :], dest_hot, (((0,), (0,)), ((), ())),
        preferred_element_type=F32, precision=lax.Precision.HIGHEST,
    )
    hit = iota((back_ref.shape[2], rows), 0) == meta[1:2, :]
    keep_ref[...] = jnp.sum(jnp.where(hit, spread, 0.0), axis=0, keepdims=True)


def all_pairs(arrived, arrived_tags, validity, block_size):
    slot_count, feature_width = arrived.shape
    block_count = slot_count // block_size

    def score_block(pieces):
        block_rows, block_tags = pieces
        gram = jnp.einsum("rd,qd->rq", block_rows, arrived, preferred_element_type=jnp.float32)
        same_cluster = (block_tags[:, None] == arrived_tags[None, :]) & validity[None, :]
        similar = jnp.sum(jnp.where(same_cluster, gram, 0.0), axis=1)
        density = jnp.sum(jnp.where(same_cluster, jnp.exp(SHARPNESS * (gram - 1.0)), 0.0), axis=1)
        return (similar, density)

    similar, density = lax.map(
        score_block,
        (
            arrived.reshape(block_count, block_size, feature_width),
            arrived_tags.reshape(block_count, block_size),
        ),
    )
    return (similar.reshape(slot_count), density.reshape(slot_count))


def full_capacity(embeddings, assignment, owner_map):
    row_count, feature_width = embeddings.shape
    devices = lax.axis_size("samp") * lax.axis_size("cent")
    clusters = owner_map.shape[0]
    per_owner = clusters // devices
    capacity = 4 * row_count // devices
    slot_count = devices * capacity
    unit_rows = (
        embeddings * lax.rsqrt(jnp.sum(embeddings * embeddings, axis=1, keepdims=True) + EPSILON)
    ).astype(jnp.bfloat16)
    destination = owner_map[assignment]
    cluster_order = jnp.argsort(owner_map, stable=True)
    position = (
        jnp.zeros((clusters,), jnp.int32)
        .at[cluster_order]
        .set(jnp.arange(clusters, dtype=jnp.int32))
    )
    local_rank = position[assignment] - destination * per_owner
    dest_onehot = (destination[:, None] == jnp.arange(devices, dtype=jnp.int32)[None, :]).astype(
        jnp.int32
    )
    within_rank = jnp.sum(jnp.cumsum(dest_onehot, axis=0) * dest_onehot, axis=1) - 1
    slot_index = destination * capacity + within_rank
    outgoing = jnp.zeros((slot_count, feature_width), jnp.bfloat16).at[slot_index].set(unit_rows)
    labels = (
        jnp.zeros((slot_count,), jnp.bfloat16)
        .at[slot_index]
        .set((local_rank + 1).astype(jnp.bfloat16))
    )
    arrived, arrived_labels = (
        lax.all_to_all(outgoing, ("samp", "cent"), split_axis=0, concat_axis=0, tiled=True),
        lax.all_to_all(labels, ("samp", "cent"), split_axis=0, concat_axis=0, tiled=True),
    )
    arrived_tags = arrived_labels.astype(jnp.int32) - 1
    validity = arrived_tags >= 0
    block_size = min(512, slot_count)
    similar, density = all_pairs(arrived, arrived_tags, validity, block_size)
    member = arrived_tags[None, :] == jnp.arange(per_owner, dtype=jnp.int32)[:, None]
    member_bf = member.astype(jnp.bfloat16)
    cluster_sums = jnp.dot(member_bf, arrived, preferred_element_type=jnp.float32)
    inverse_norm = lax.rsqrt(jnp.sum(cluster_sums * cluster_sums, axis=1) + EPSILON)
    row_scale = jnp.sum(member.astype(jnp.float32) * inverse_norm[:, None], axis=0)
    spread = 1.0 - similar * row_scale
    weight = jnp.where(validity, jnp.exp(spread) / jnp.where(validity, density, 1.0), 0.0)
    weighted = jnp.dot(
        member_bf * weight.astype(jnp.bfloat16)[None, :],
        arrived,
        preferred_element_type=jnp.float32,
    )
    centroid = cluster_sums * inverse_norm[:, None]
    representative = weighted * lax.rsqrt(
        jnp.sum(weighted * weighted, axis=1, keepdims=True) + EPSILON
    )
    returned = lax.all_to_all(weight, ("samp", "cent"), split_axis=0, concat_axis=0, tiled=True)
    keep_weight = returned[slot_index]
    return (centroid, representative, keep_weight)


def on_device(embeddings, assignment, owner_map):
    rows, width = embeddings.shape
    n_samp = lax.axis_size("samp")
    n_cent = lax.axis_size("cent")
    devices = n_samp * n_cent
    clusters = owner_map.shape[0]
    per_owner = clusters // devices
    capacity = 4 * rows // devices
    near = capacity // 2
    pool = capacity - near
    vmem = pl.BlockSpec(memory_space=pltpu.VMEM)
    anywhere = pl.BlockSpec(memory_space=pl.ANY)
    shape = jax.ShapeDtypeStruct
    dma = pltpu.SemaphoreType.DMA
    block = n_samp * near
    blocks = n_cent + n_samp // 2
    slots = blocks * block
    limit = 21 * block // 32 // 8 * 8
    room = (limit + LANES - 1) // LANES * LANES
    send, pooled, index, labels, meta = pl.pallas_call(
        functools.partial(pack_kernel, devices, n_cent, near, pool),
        out_shape=(
            shape((n_cent, limit, width), BF),
            shape((pool, width), BF),
            shape((n_cent, 1, room), F32),
            shape((devices, 1, 2 * block), F32),
            shape((8, rows), jnp.int32),
        ),
        in_specs=[vmem] * 3,
        out_specs=(vmem,) * 5,
        name="pack",
    )(embeddings, assignment.reshape(1, rows), owner_map.reshape(1, clusters))
    centroid, representative, back, tags = pl.pallas_call(
        functools.partial(dedup_kernel, n_samp, n_cent),
        out_shape=(
            shape((per_owner, width), F32),
            shape((per_owner, width), F32),
            shape((devices, 1, 2 * block), F32),
            shape((blocks, 1, block), F32),
        ),
        in_specs=[anywhere] * 4,
        out_specs=(vmem,) * 4,
        scratch_shapes=[
            pltpu.VMEM((n_cent, limit, width), BF),
            pltpu.VMEM((n_cent, 1, room), F32),
            pltpu.VMEM((n_cent, n_samp, near, width), BF),
            pltpu.VMEM((n_cent, n_samp, near, width), BF),
            pltpu.VMEM((n_samp, n_cent, pool, width), BF),
            pltpu.VMEM((n_samp, n_cent, 1, 2 * block), F32),
            pltpu.VMEM((slots, width), BF),
            pltpu.VMEM((slots, LANES), F32),
            pltpu.VMEM((slots, LANES), F32),
            pltpu.VMEM((blocks, 1, block), F32),
            pltpu.VMEM((per_owner, width), F32),
            pltpu.VMEM((n_cent, n_samp // 2, 1, 2 * block), F32),
            dma((5,)),
            dma((n_samp, n_cent)), dma((n_samp, n_cent)), dma((n_samp, n_cent)), dma((n_samp, n_cent)),
            dma((n_cent,)), dma((n_cent,)), dma((n_samp,)), dma((n_samp,)),
            dma((n_samp, n_cent)), dma((n_samp, n_cent)),
            dma((n_cent,)), dma((n_cent,)), dma((n_cent,)), dma((n_cent,)), dma((n_samp,)),
        ],
        compiler_params=pltpu.CompilerParams(collective_id=0, has_side_effects=True),
        name="dedup",
    )(send, pooled, index, labels)
    keep, top = pl.pallas_call(
        pick_kernel,
        out_shape=(shape((1, rows), F32), shape((1, 1), F32)),
        in_specs=[vmem] * 3,
        out_specs=(vmem, pl.BlockSpec(memory_space=pltpu.SMEM)),
        name="pick",
    )(back, meta, tags)
    keep = keep.reshape(rows)

    def fast(embeddings, assignment, owner_map, centroid, representative, keep):
        return centroid, representative, keep

    def slow(embeddings, assignment, owner_map, centroid, representative, keep):
        return full_capacity(embeddings, assignment, owner_map)

    spilled = top[0, 0] >= SPILL
    return lax.cond(
        spilled, slow, fast, embeddings, assignment, owner_map, centroid, representative, keep
    )


def solution(mesh):
    in_specs = (P(("samp", "cent"), None), P(("samp", "cent")), P())
    out_specs = (P(("samp", "cent"), None), P(("samp", "cent"), None), P(("samp", "cent")))
    return jax.shard_map(
        on_device, mesh=mesh, in_specs=in_specs, out_specs=out_specs, check_vma=False
    )
```
